32 devices in a mesh: strip: 4 (over y, x), depth: 8 (over z, core).
Axes of the slice: x: 2, y: 2, z: 4, core: 2. Of those that a mesh axis runs over, the one named last changes fastest.
Arguments:
- volume: bfloat16 [64, 128, 2048], P('depth', 'strip'), may hold values from -6 to 6
- occupancy: int32 [8, 4, 16], P('depth', 'strip'), may hold values from 0 to 1
- slab_order: int32 [8], replicated, may hold values from 0 to 7, as said below
- w_in: bfloat16 [4, 64], replicated, may hold values from -3 to 3
- b_in: float32 [64], replicated, may hold values from -3 to 3
- w_out: bfloat16 [64, 4], replicated, may hold values from -1.5 to 1.5
- b_out: float32 [4], replicated, may hold values from -3 to 3
- conv_weight: float32 [3, 3, 3, 3], replicated, may hold values from -1.25 to 1.25
- conv_bias: float32 [3], replicated, may hold values from -3 to 3
Outputs:
- denoised: float32 [3, 4, 4, 8, 2048], P(None, 'strip', None, 'depth')
The draws below stay inside these ranges and needn't reach their ends.
Inputs may be any that keep to these rules, and one draw needn't show every extreme that they name: slab_order is a permutation; for every bit b, bit b of slab_order[d] is bit b of d XOR a value that depends only on d's bits above b (so slabs that agree on their bits above b hold consecutive positions).
All inputs are finite; a program needn't handle non-finite values.
Results may differ from the reference program's by a relative error of at most 0.0003.
Values may be sent and summed in bfloat16 or wider, within the bound.
A program may use at most 64 MiB of HBM per device.

```python
import jax
import jax.numpy as jnp
from jax import lax

WIDTH = 2048
Z_DEV = 8
CHANNELS = 4
HIDDEN_SIZE = 64
BRICK_ROWS = 32
BRICK_COLS = 128
HEIGHT = 128
DEPTH = 64
ROW_SHARE = 4
N_STRIP = 4
N_DEPTH = 8


def draw_occupancy(key, part):
    level_key = jax.random.fold_in(key, 11)
    value_key = jax.random.fold_in(key, 12)
    levels = jax.random.randint(level_key, (N_DEPTH, 1, 1), 2, 9)
    values = jax.random.randint(value_key, (N_DEPTH, HEIGHT // BRICK_ROWS, WIDTH // BRICK_COLS), 0, 8)
    return (values < levels).astype(jnp.int32)


def draw_slab_order(key, part):
    indices = jnp.arange(N_DEPTH, dtype=jnp.int32)
    order_now = indices
    bit_total = N_DEPTH.bit_length() - 1
    for bit_index in range(bit_total):
        flips = jax.random.randint(jax.random.fold_in(key, 30 + bit_index), (N_DEPTH,), 0, 2).astype(jnp.int32)
        chosen = jnp.take(flips, jnp.right_shift(indices, bit_index + 1))
        order_now = jnp.bitwise_xor(order_now, jnp.left_shift(chosen, bit_index)).astype(jnp.int32)
    return order_now.astype(jnp.int32)


def steps_of(rng, dims, shards, low, high):
    gain = 1.0
    for dim, shards_of in shards:
        draws = jax.random.uniform(jax.random.fold_in(jax.random.fold_in(rng, 6), dim), (shards_of,), jnp.float32, low / len(shards), high / len(shards))
        gain = gain * jnp.repeat(jnp.exp(draws), dims[dim] // shards_of).reshape((-1,) + (1,) * (len(dims) - 1 - dim))
    return gain


def bell_draw(rng, dims, scale, bound, pieces=(), kind=jnp.bfloat16):
    entries = scale * jax.random.normal(rng, dims, jnp.float32)
    if pieces:
        entries = entries * steps_of(rng, dims, pieces, -0.22, 0.18)
    return jnp.clip(entries, -bound, bound).astype(kind)


def setup_inputs(seed: int = 0) -> dict:
    seeds = jax.random.split(jax.random.key(seed), 10)
    volume = bell_draw(seeds[0], (DEPTH, HEIGHT, WIDTH), 1.0, 6.0, ((0, 8), (1, 4)))
    occupancy = draw_occupancy(jax.random.fold_in(seeds[9], 71), 0)
    slab_order = draw_slab_order(jax.random.fold_in(seeds[9], 71), 0)
    w_in = bell_draw(seeds[3], (CHANNELS, HIDDEN_SIZE), CHANNELS ** -0.5, 3.0)
    b_in = bell_draw(seeds[4], (HIDDEN_SIZE,), 0.5, 3.0, (), jnp.float32)
    w_out = bell_draw(seeds[5], (HIDDEN_SIZE, CHANNELS), 0.25, 1.5)
    b_out = bell_draw(seeds[6], (CHANNELS,), 1.0, 3.0, (), jnp.float32)
    conv_weight = bell_draw(seeds[7], (3, 3, 3, 3), 27 ** -0.5, 1.25, (), jnp.float32)
    conv_bias = bell_draw(seeds[8], (3,), 0.5, 3.0, (), jnp.float32)
    return dict(volume=volume, occupancy=occupancy, slab_order=slab_order, w_in=w_in, b_in=b_in, w_out=w_out, b_out=b_out, conv_weight=conv_weight, conv_bias=conv_bias)


def expand_bricks(bricks):
    brick_rows_n, brick_cols_n = bricks.shape
    spread = jnp.broadcast_to(bricks.astype(jnp.float32)[:, None, :, None], (brick_rows_n, BRICK_ROWS, brick_cols_n, BRICK_COLS))
    return spread.reshape(brick_rows_n * BRICK_ROWS, brick_cols_n * BRICK_COLS)


def march_slab(features, coverage, w_in, b_in, w_out, b_out, optical):
    rows_all = features.shape[2]
    cols_all = features.shape[3]

    def layer_step(state_pair, layer_feats):
        colour_sum, remaining = state_pair
        flattened = layer_feats.reshape(4, rows_all * cols_all)
        hidden = jax.nn.silu(jnp.dot(w_in.T, flattened, preferred_element_type=jnp.float32) + b_in[:, None]).astype(jnp.bfloat16)
        output = jnp.dot(w_out.T, hidden, preferred_element_type=jnp.float32) + b_out[:, None]
        output = output.reshape(4, rows_all, cols_all)
        colour = jax.nn.sigmoid(output[:3])
        density = jax.nn.softplus(output[3]) * coverage
        alpha_val = 1.0 - jnp.exp(-optical * density)
        colour_sum = colour_sum + (remaining * alpha_val)[None] * colour
        remaining = remaining * (1.0 - alpha_val)
        return (colour_sum, remaining), None

    start = (jnp.zeros((3, rows_all, cols_all), jnp.float32), jnp.ones((rows_all, cols_all), jnp.float32))
    (colour_sum, remaining), unused = lax.scan(layer_step, start, features)
    return colour_sum, remaining


def slab_features(slab_field):
    scalar_field = slab_field.astype(jnp.float32)
    padded_cols = jnp.pad(scalar_field, ((0, 0), (0, 0), (1, 1)))
    grad_cols = 0.5 * (padded_cols[:, :, 2:] - padded_cols[:, :, :-2])
    padded_rows = jnp.pad(scalar_field, ((0, 0), (1, 1), (0, 0)))
    grad_rows = 0.5 * (padded_rows[:, 2:] - padded_rows[:, :-2])
    padded_depth = jnp.concatenate([scalar_field[:1], scalar_field, scalar_field[-1:]], 0)
    grad_depth = 0.5 * (padded_depth[2:] - padded_depth[:-2])
    return jnp.stack([scalar_field, grad_cols, grad_rows, grad_depth], 1).astype(jnp.bfloat16)


def denoise(picture, conv_weight, conv_bias):
    rows_all = picture.shape[1]
    cols_all = picture.shape[2]
    padded = jnp.pad(picture, ((0, 0), (1, 1), (1, 1)))
    filtered = jnp.broadcast_to(conv_bias[:, None, None], (3, rows_all, cols_all))
    for row_off in range(3):
        for col_off in range(3):
            window = padded[:, row_off:row_off + rows_all, col_off:col_off + cols_all]
            filtered = filtered + jnp.sum(conv_weight[:, :, row_off, col_off][:, :, None, None] * window[None], axis=1)
    return filtered


def reference(volume, occupancy, slab_order, w_in, b_in, w_out, b_out, conv_weight, conv_bias):
    optical = 2.0 / DEPTH
    inverse = jnp.argsort(slab_order).astype(jnp.int32)

    def composite(state_pair, position):
        colour_acc, remaining_acc = state_pair
        slab_index = inverse[position].astype(jnp.int32)
        slab_field = lax.dynamic_slice_in_dim(volume, (slab_index * Z_DEV).astype(jnp.int32), Z_DEV, 0)
        coverage = expand_bricks(lax.dynamic_index_in_dim(occupancy, slab_index, 0, keepdims=False))
        colour_slab, remaining_slab = march_slab(slab_features(slab_field), coverage, w_in, b_in, w_out, b_out, optical)
        return (colour_acc + remaining_acc[None] * colour_slab, remaining_acc * remaining_slab), None

    start = (jnp.zeros((3, HEIGHT, WIDTH), jnp.float32), jnp.ones((HEIGHT, WIDTH), jnp.float32))
    (picture, remaining_end), unused = lax.scan(composite, start, jnp.arange(N_DEPTH, dtype=jnp.int32))
    filtered = denoise(picture, conv_weight, conv_bias)
    return filtered.reshape(3, N_STRIP, ROW_SHARE, N_DEPTH, WIDTH)
```

```python
import functools

import jax
import jax.numpy as jnp
from jax import lax
from jax.experimental import pallas as pl
from jax.experimental.pallas import tpu as pltpu
from jax.sharding import PartitionSpec as P

MESH = pl.DeviceIdType.MESH
LANES = 128
WIDE = 2 * LANES
F32 = jnp.float32
BF16 = jnp.bfloat16


def iota(shape, dim):
    return lax.broadcasted_iota(jnp.int32, shape, dim)


def over(in_front, mine, theirs):
    front = [jnp.where(in_front, a, b) for a, b in zip(mine, theirs)]
    back = [jnp.where(in_front, b, a) for a, b in zip(mine, theirs)]
    colour = [front[i] + front[3] * back[i] for i in range(3)]
    return colour + [mine[3] * theirs[3]]


def render_kernel(
    strips, depths, unroll,
    occ_ref, order_ref, b_out_ref, conv_ref, conv_bias_ref, w_in_ref, b_in_ref, w_out_ref, vol_hbm,
    out_ref,
    vol, feat, hid_a, hid_b, lhs, mix, square, part, edge_top, edge_bottom, above, below,
    pic, up, down, up_strip, down_strip, *rest,
):
    rounds = depths.bit_length() - 1
    sends, receives, currents = rest[:rounds], rest[rounds:2 * rounds], rest[2 * rounds:3 * rounds]
    vol_sem, edge_sems, swap_send, swap_recv, pic_send, pic_recv = rest[3 * rounds:]
    layers, rows, cols = vol.shape
    tiles = rows // 8
    hidden = w_in_ref.shape[1]
    half = 4 * hidden
    chunks = cols // WIDE
    brick = cols // occ_ref.shape[0]
    share = rows // depths
    optical = 2.0 / (layers * depths)
    s = lax.axis_index("strip")
    d = lax.axis_index("depth")

    load = pltpu.make_async_copy(vol_hbm, vol, vol_sem)
    load.start()

    for ref in (above, below):
        ref[...] = jnp.zeros(ref.shape, F32)
    for ref in (up_strip, down_strip, pic):
        ref[...] = jnp.zeros(ref.shape, F32)

    barrier = pltpu.get_barrier_semaphore()

    def greet(strip, depth):
        pl.semaphore_signal(barrier, inc=1, device_id=(strip, depth), device_id_type=MESH)

    next_d = lax.rem(d + 1, depths)
    last_d = lax.rem(d + depths - 1, depths)
    for r in range(rounds):
        greet(s, d ^ (1 << r))
    greet(s, next_d)
    greet(s, last_d)
    has_above, has_below = s > 0, s < strips - 1
    at_first, at_last = d == 0, d == depths - 1
    corner_above = jnp.logical_and(at_first, has_above)
    corner_below = jnp.logical_and(at_last, has_below)

    @pl.when(has_above)
    def _():
        greet(s - 1, d)

    @pl.when(has_below)
    def _():
        greet(s + 1, d)

    @pl.when(corner_above)
    def _():
        greet(s - 1, depths - 1)

    @pl.when(corner_below)
    def _():
        greet(s + 1, 0)

    square[...] = jnp.zeros(square.shape, F32)
    rest_bias = 0.5 * b_in_ref[...]
    square[0, 0:4, 0:hidden] = 0.5 * w_in_ref[...].astype(F32)
    for k in range(3):
        piece = rest_bias.astype(BF16).astype(F32)
        square[0, 4 + k:5 + k, 0:hidden] = piece
        rest_bias = rest_bias - piece
    square[1, 0:hidden, 0:4] = w_out_ref[...].astype(F32)
    turned = square[0].T.astype(BF16)
    depth_lhs = lhs.shape[1]
    for row in range(8):
        k = iota((128, depth_lhs), 0)
        at = iota((128, depth_lhs), 1)
        place = jnp.where(k < 4, k * 8 + row, jnp.where(k < 7, 28 + k, -1))
        chosen = jnp.where(at == place, 1.0, 0.0).astype(BF16)
        picked = jnp.dot(turned, chosen, preferred_element_type=F32)
        lhs[row * hidden:(row + 1) * hidden] = picked[:hidden].astype(BF16)
    out_turned = square[1].T
    scale = jnp.where(iota(out_turned.shape, 0) < 3, 0.5, 1.0)
    out_turned = (out_turned * scale).astype(BF16)
    spread = jnp.where(iota((128, half), 1) % hidden == iota((128, half), 0), 1.0, 0.0).astype(BF16)
    spread = jnp.dot(out_turned, spread, preferred_element_type=F32).astype(BF16)
    rep = jnp.where(iota((32, 128), 0) // 8 == iota((32, 128), 1), 1.0, 0.0).astype(BF16)
    base = jnp.dot(rep, spread, preferred_element_type=F32)
    for p in range(2):
        own = iota(base.shape, 1) // hidden == iota(base.shape, 0) % 8 - 4 * p
        mix[p] = jnp.where(own, base, 0.0).astype(BF16)
    out_bias = [b_out_ref[i] * (0.5 if i < 3 else 1.0) for i in range(4)]

    def clear(c, carry):
        part[c, 0:3] = jnp.zeros((3, 2, rows, LANES), F32)
        part[c, 3] = jnp.ones((2, rows, LANES), F32)
        return carry

    lax.fori_loop(0, chunks, clear, 0)
    load.wait()

    def edges(z, carry):
        edge_top[pl.ds(z, 1)] = vol[z, 0:16].astype(F32)[0:1]
        edge_bottom[pl.ds(z, 1)] = vol[z, rows - 16:rows].astype(F32)[15:16]
        return carry

    lax.fori_loop(0, layers, edges, 0)
    total_greets = (
        rounds + 2 + has_above.astype(jnp.int32) + has_below.astype(jnp.int32)
        + corner_above.astype(jnp.int32) + corner_below.astype(jnp.int32)
    )
    pl.semaphore_wait(barrier, total_greets)

    def edge_copy(source, target, which, strip):
        return pltpu.make_async_remote_copy(
            src_ref=source, dst_ref=target, send_sem=edge_sems.at[which], recv_sem=edge_sems.at[which + 2],
            device_id=(strip, d), device_id_type=MESH,
        )

    to_above = edge_copy(edge_top, below, 0, s - 1)
    to_below = edge_copy(edge_bottom, above, 1, s + 1)

    @pl.when(has_above)
    def _():
        to_above.start()

    @pl.when(has_below)
    def _():
        to_below.start()

    lane = iota((8, cols), 1)
    row8 = iota((8, cols), 0)

    def fields(z):
        here = vol[z].astype(F32)
        return here, [here[8 * t:8 * t + 8] for t in range(tiles)]

    def put_second(z, t, grad_rows, far, near):
        grad_depth = 0.5 * (far[8 * t:8 * t + 8] - near[8 * t:8 * t + 8])
        feat[z, t, 16:32] = jnp.concatenate([grad_rows, grad_depth], 0).astype(BF16)

    def near_far(z):
        far = vol[jnp.minimum(z + 1, layers - 1)].astype(F32)
        near = vol[jnp.maximum(z - 1, 0)].astype(F32)
        return far, near

    def vertical(parts, t, first, last):
        lower = parts[t + 1] if t + 1 < tiles else None
        upper = parts[t - 1] if t > 0 else None
        below_row = pltpu.roll(lower, 7, 0) if lower is not None else last
        above_row = pltpu.roll(upper, 1, 0) if upper is not None else first
        following = jnp.where(row8 == 7, below_row, pltpu.roll(parts[t], 7, 0))
        previous = jnp.where(row8 == 0, above_row, pltpu.roll(parts[t], 1, 0))
        return 0.5 * (following - previous)

    ones = jnp.ones((16, cols), BF16)

    def inner_features(z, carry):
        here, parts = fields(z)
        far, near = near_far(z)
        for t in range(tiles):
            right = jnp.where(lane == cols - 1, 0.0, pltpu.roll(parts[t], cols - 1, 1))
            left = jnp.where(lane == 0, 0.0, pltpu.roll(parts[t], 1, 1))
            feat[z, t, 0:16] = jnp.concatenate([parts[t], 0.5 * (right - left)], 0).astype(BF16)
            if 0 < t < tiles - 1:
                put_second(z, t, vertical(parts, t, None, None), far, near)
            feat[z, t, 32:48] = ones
        return carry

    lax.fori_loop(0, layers, inner_features, 0)

    @pl.when(has_above)
    def _():
        to_below.wait_recv()

    @pl.when(has_below)
    def _():
        to_above.wait_recv()

    def outer_features(z, carry):
        here, parts = fields(z)
        far, near = near_far(z)
        first = jnp.broadcast_to(above[pl.ds(z, 1)], (8, cols))
        last = jnp.broadcast_to(below[pl.ds(z, 1)], (8, cols))
        for t in (0, tiles - 1):
            put_second(z, t, vertical(parts, t, first, last), far, near)
        return carry

    lax.fori_loop(0, layers, outer_features, 0)

    def both(n, fresh, ready):
        z, c = lax.rem(n, layers), n // layers
        before = jnp.maximum(n - 1, 0)
        c2 = before // layers
        into = jnp.where(n > 0, c2, chunks)
        at = pl.multiple_of(jnp.minimum(c, chunks - 1) * WIDE, WIDE)
        cover = jnp.concatenate(
            [
                jnp.full((8, brick), occ_ref[c2 * (WIDE // brick) + b].astype(F32))
                for b in range(WIDE // brick)
            ],
            1,
        )
        for pair in range(0, tiles, 2):
            outs = [[], []]
            for p in range(2):
                if fresh is not None:
                    for t in range(2):
                        x = feat[z, pair + t, :, pl.ds(at, WIDE)]
                        u = jnp.dot(lhs[p * half:(p + 1) * half], x, preferred_element_type=F32)
                        fresh[pair + t, p] = (u + u * jnp.tanh(u)).astype(BF16)
                for t in range(2):
                    outs[t].append(jnp.dot(mix[p], ready[pair + t, p], preferred_element_type=F32))
            for t in range(2):
                out = outs[t][0] + outs[t][1]
                raw = out[24:32] + out_bias[3]
                density = jnp.maximum(raw, 0.0) + jnp.log(1.0 + jnp.exp(-jnp.abs(raw)))
                keep = jnp.exp(-optical * (density * cover))
                here = pl.ds(8 * (pair + t), 8)
                glow = [jnp.tanh(out[8 * i:8 * i + 8] + out_bias[i]) for i in range(3)]
                for w in range(2):
                    lanes = slice(w * LANES, (w + 1) * LANES)
                    remaining = part[into, 3, w, here]
                    weight = 0.5 * (remaining * (1.0 - keep[:, lanes]))
                    for i in range(3):
                        part[into, i, w, here] = part[into, i, w, here] + (weight + weight * glow[i][:, lanes])
                    part[into, 3, w, here] = remaining * keep[:, lanes]

    own_order = order_ref[d]

    def swap(r, c):
        return pltpu.make_async_remote_copy(
            src_ref=sends[r].at[c], dst_ref=receives[r].at[c],
            send_sem=swap_send.at[r, c], recv_sem=swap_recv.at[r, c],
            device_id=(s, d ^ (1 << r)), device_id_type=MESH,
        )

    def pic_copy(c, which, target, strip, depth):
        at = pl.ds(pl.multiple_of(c * WIDE, WIDE), WIDE)
        return pltpu.make_async_remote_copy(
            src_ref=pic.at[:, :, at], dst_ref=target.at[:, :, at],
            send_sem=pic_send.at[which, c], recv_sem=pic_recv.at[which, c],
            device_id=(strip, depth), device_id_type=MESH,
        )

    def pic_copies(c):
        return [
            (None, None, pic_copy(c, 0, up, s, next_d)),
            (None, None, pic_copy(c, 1, down, s, last_d)),
            (corner_below, corner_above, pic_copy(c, 2, up_strip, s + 1, 0)),
            (corner_above, corner_below, pic_copy(c, 3, down_strip, s - 1, depths - 1)),
        ]

    def when(condition, action):
        if condition is None:
            action()
        else:
            pl.when(condition)(action)

    def split(ref, c, i, w, r):
        count = rows >> (r + 1)
        even = ref[c, i, w, pl.ds(0, count, stride=2)]
        odd = ref[c, i, w, pl.ds(1, count, stride=2)]
        mine_odd = ((d >> r) & 1) == 1
        return jnp.where(mine_odd, odd, even), jnp.where(mine_odd, even, odd)

    def progress(r, c):
        source = part if r <= 1 else currents[r - 2]
        if r > 0:
            swap(r - 1, c).wait_recv()
            in_front = ((own_order >> (r - 1)) & 1) == 0
            for w in range(2):
                mine = [split(source, c, i, w, r - 1)[0] for i in range(4)]
                theirs = [receives[r - 1][c, i, w] for i in range(4)]
                fresh = over(in_front, mine, theirs)
                if r < rounds:
                    for i in range(4):
                        currents[r - 1][c, i, w] = fresh[i]
                else:
                    at = pl.ds(pl.multiple_of(c * WIDE + w * LANES, LANES), LANES)
                    for i in range(3):
                        pic[i, 0:share, at] = fresh[i]
        if r < rounds:
            source = part if r == 0 else currents[r - 1]
            for i in range(4):
                for w in range(2):
                    sends[r][c, i, w] = split(source, c, i, w, r)[1]
            swap(r, c).start()
        else:
            for sending, unused, copy in pic_copies(c):
                when(sending, copy.start)

    bodies = layers // unroll

    def advance(m, static):
        for r in range(rounds, -1, -1):
            if static:
                if (m - r) % bodies == 0 and 0 <= (m - r) // bodies - 1 < chunks:
                    progress(r, (m - r) // bodies - 1)
            else:
                c = (m - r) // bodies - 1
                ready = jnp.logical_and(lax.rem(m - r + rounds * bodies, bodies) == 0, m >= r + bodies)

                @pl.when(ready)
                def _():
                    progress(r, c)

    def body(m, carry):
        for k in range(unroll):
            if k % 2 == 0:
                both(m * unroll + k, hid_a, hid_b)
            else:
                both(m * unroll + k, hid_b, hid_a)
        advance(m, False)
        return carry

    lax.fori_loop(0, chunks * bodies, body, 0)
    both(chunks * layers, None, hid_b)
    for m in range(chunks * bodies, chunks * bodies + rounds + 1):
        advance(m, True)

    def settle(c, carry):
        for r in range(rounds):
            swap(r, c).wait_send()
        for sending, receiving, copy in pic_copies(c):
            when(sending, copy.wait_send)
            when(receiving, copy.wait_recv)
        return carry

    lax.fori_loop(0, chunks, settle, 0)

    @pl.when(has_above)
    def _():
        to_above.wait_send()

    @pl.when(has_below)
    def _():
        to_below.wait_send()

    total = [jnp.full((8, cols), conv_bias_ref[o]) for o in range(3)]
    for i in range(3):
        upper, lower = up[i], down[i]
        first = jnp.where(row8 == 0, pltpu.roll(up_strip[i], (9 - share) % 8, 0), pltpu.roll(upper, 1, 0))
        upper = jnp.where(at_first, first, upper)
        last = jnp.where(row8 == share - 1, pltpu.roll(down_strip[i], share - 1, 0), pltpu.roll(lower, 7, 0))
        lower = jnp.where(at_last, last, lower)
        for a, centre in enumerate((upper, pic[i], lower)):
            left = jnp.where(lane == 0, 0.0, pltpu.roll(centre, 1, 1))
            right = jnp.where(lane == cols - 1, 0.0, pltpu.roll(centre, cols - 1, 1))
            for b, window in enumerate((left, centre, right)):
                for o in range(3):
                    total[o] = total[o] + conv_ref[((o * 3 + i) * 3 + a) * 3 + b] * window
    for o in range(3):
        out_ref[o] = total[o][0:share]


def shards(volume, occupancy, slab_order, w_in, b_in, w_out, b_out, conv_weight, conv_bias):
    strips, depths = lax.axis_size("strip"), lax.axis_size("depth")
    layers, rows, cols = volume.shape
    channels, hidden = w_in.shape
    rounds = depths.bit_length() - 1
    chunks = cols // WIDE
    tiles = rows // 8
    share = rows // depths
    smem = pl.BlockSpec(memory_space=pltpu.SMEM)
    vmem = pl.BlockSpec(memory_space=pltpu.VMEM)
    depth_lhs = channels * 8 + 16
    halves = [pltpu.VMEM((chunks, 4, 2, rows >> (r + 1), LANES), F32) for r in range(rounds)]
    picture = pltpu.VMEM((3, 8, cols), F32)
    edge = pltpu.VMEM((layers, cols), F32)
    dma = pltpu.SemaphoreType.DMA
    unroll = 4 if layers % 4 == 0 else 2
    result = pl.pallas_call(
        functools.partial(render_kernel, strips, depths, unroll),
        out_shape=jax.ShapeDtypeStruct((3, share, cols), F32),
        in_specs=[smem] * 5 + [vmem] * 3 + [pl.BlockSpec(memory_space=pl.ANY)],
        out_specs=vmem,
        scratch_shapes=[
            pltpu.VMEM((layers, rows, cols), BF16),
            pltpu.VMEM((layers, tiles, depth_lhs, cols), BF16),
            pltpu.VMEM((tiles, 2, 4 * hidden, WIDE), BF16),
            pltpu.VMEM((tiles, 2, 4 * hidden, WIDE), BF16),
            pltpu.VMEM((8 * hidden, depth_lhs), BF16),
            pltpu.VMEM((2, 32, 4 * hidden), BF16),
            pltpu.VMEM((2, 128, 128), F32),
            pltpu.VMEM((chunks + 1, 4, 2, rows, LANES), F32),
            edge, edge, edge, edge,
            picture, picture, picture, picture, picture,
            *halves, *halves, *halves,
            dma(()), dma((4,)), dma((rounds, chunks)), dma((rounds, chunks)), dma((4, chunks)), dma((4, chunks)),
        ],
        compiler_params=pltpu.CompilerParams(
            collective_id=0, has_side_effects=True, vmem_limit_bytes=48 * 1024 * 1024
        ),
        name="render",
    )(
        occupancy.reshape(-1), slab_order, b_out, conv_weight.reshape(-1), conv_bias,
        w_in, b_in.reshape(1, hidden), w_out, volume,
    )
    return result.reshape(3, 1, share, 1, cols)


def solution(mesh):
    placed = (P("depth", "strip", None), P("depth", "strip", None)) + (P(),) * 7
    return jax.shard_map(
        shards,
        mesh=mesh,
        in_specs=placed,
        out_specs=P(None, "strip", None, "depth", None),
        check_vma=False,
    )
```

```python
import functools

import jax
import jax.numpy as jnp
from jax import lax
from jax.experimental import pallas as pl
from jax.experimental.pallas import tpu as pltpu
from jax.sharding import PartitionSpec as P

MESH = pl.DeviceIdType.MESH
LANES = 128
WIDE = 2 * LANES
F32 = jnp.float32
BF16 = jnp.bfloat16


def iota(shape, dim):
    return lax.broadcasted_iota(jnp.int32, shape, dim)


def over(in_front, mine, theirs):
    front = [jnp.where(in_front, a, b) for a, b in zip(mine, theirs)]
    back = [jnp.where(in_front, b, a) for a, b in zip(mine, theirs)]
    colour = [front[i] + front[3] * back[i] for i in range(3)]
    return colour + [mine[3] * theirs[3]]


def render_kernel(
    strips, depths, gap,
    occ_ref, order_ref, b_out_ref, conv_ref, conv_bias_ref, w_in_ref, b_in_ref, w_out_ref, vol_hbm,
    out_ref,
    vol, feat, hid_a, hid_b, lhs, mix, square, part, edge_top, edge_bottom, above, below,
    pic, up, down, up_strip, down_strip, *rest,
):
    rounds = depths.bit_length() - 1
    sends, receives, currents = rest[:rounds], rest[rounds:2 * rounds], rest[2 * rounds:3 * rounds]
    vol_sem, edge_sems, swap_send, swap_recv, pic_send, pic_recv = rest[3 * rounds:]
    layers, rows, cols = vol.shape
    tiles = rows // 8
    hidden = w_in_ref.shape[1]
    half = 4 * hidden
    chunks = cols // WIDE
    brick = cols // occ_ref.shape[0]
    share = rows // depths
    optical = 2.0 / (layers * depths)
    s = lax.axis_index("strip")
    d = lax.axis_index("depth")

    load = pltpu.make_async_copy(vol_hbm, vol, vol_sem)
    load.start()

    for ref in (above, below):
        ref[...] = jnp.zeros(ref.shape, F32)
    for ref in (up_strip, down_strip, pic):
        ref[...] = jnp.zeros(ref.shape, F32)

    barrier = pltpu.get_barrier_semaphore()

    def greet(strip, depth):
        pl.semaphore_signal(barrier, inc=1, device_id=(strip, depth), device_id_type=MESH)

    next_d = lax.rem(d + 1, depths)
    last_d = lax.rem(d + depths - 1, depths)
    for r in range(rounds):
        greet(s, d ^ (1 << r))
    greet(s, next_d)
    greet(s, last_d)
    has_above, has_below = s > 0, s < strips - 1
    at_first, at_last = d == 0, d == depths - 1
    corner_above = jnp.logical_and(at_first, has_above)
    corner_below = jnp.logical_and(at_last, has_below)

    @pl.when(has_above)
    def _():
        greet(s - 1, d)

    @pl.when(has_below)
    def _():
        greet(s + 1, d)

    @pl.when(corner_above)
    def _():
        greet(s - 1, depths - 1)

    @pl.when(corner_below)
    def _():
        greet(s + 1, 0)

    def when(condition, action):
        if condition is None:
            action()
        else:
            pl.when(condition)(action)

    square[...] = jnp.zeros(square.shape, F32)
    rest_bias = 0.5 * b_in_ref[...]
    square[0, 0:4, 0:hidden] = 0.5 * w_in_ref[...].astype(F32)
    for k in range(3):
        piece = rest_bias.astype(BF16).astype(F32)
        square[0, 4 + k:5 + k, 0:hidden] = piece
        rest_bias = rest_bias - piece
    square[1, 0:4, 0:hidden] = w_out_ref[...].astype(F32)
    turned = square[0].T.astype(BF16)
    depth_lhs = lhs.shape[1]
    for row in range(8):
        k = iota((128, depth_lhs), 0)
        at = iota((128, depth_lhs), 1)
        place = jnp.where(k < 4, k * 8 + row, jnp.where(k < 7, 28 + k, -1))
        chosen = jnp.where(at == place, 1.0, 0.0).astype(BF16)
        picked = jnp.dot(turned, chosen, preferred_element_type=F32)
        lhs[row * hidden:(row + 1) * hidden] = picked[:hidden].astype(BF16)
    out_turned = square[1]
    scale = jnp.where(iota(out_turned.shape, 0) < 3, 0.5, 1.0)
    out_turned = (out_turned * scale).astype(BF16)
    spread = jnp.where(iota((128, half), 1) % hidden == iota((128, half), 0), 1.0, 0.0).astype(BF16)
    spread = jnp.dot(out_turned, spread, preferred_element_type=F32).astype(BF16)
    rep = jnp.where(iota((32, 128), 0) // 8 == iota((32, 128), 1), 1.0, 0.0).astype(BF16)
    base = jnp.dot(rep, spread, preferred_element_type=F32)
    for p in range(2):
        own = iota(base.shape, 1) // hidden == iota(base.shape, 0) % 8 - 4 * p
        mix[p] = jnp.where(own, base, 0.0).astype(BF16)
    out_bias = [b_out_ref[i] * (0.5 if i < 3 else 1.0) for i in range(4)]

    def clear(c, carry):
        part[c, 0:3] = jnp.zeros((3, 2, rows, LANES), F32)
        part[c, 3] = jnp.ones((2, rows, LANES), F32)
        return carry

    lax.fori_loop(0, chunks, clear, 0)
    load.wait()

    def edges(z, carry):
        edge_top[pl.ds(z, 1)] = vol[z, 0:16].astype(F32)[0:1]
        edge_bottom[pl.ds(z, 1)] = vol[z, rows - 16:rows].astype(F32)[15:16]
        return carry

    lax.fori_loop(0, layers, edges, 0)
    total_greets = (
        rounds + 2 + has_above.astype(jnp.int32) + has_below.astype(jnp.int32)
        + corner_above.astype(jnp.int32) + corner_below.astype(jnp.int32)
    )

    def edge_copy(source, target, which, strip):
        return pltpu.make_async_remote_copy(
            src_ref=source, dst_ref=target, send_sem=edge_sems.at[which], recv_sem=edge_sems.at[which + 2],
            device_id=(strip, d), device_id_type=MESH,
        )

    to_above = edge_copy(edge_top, below, 0, s - 1)
    to_below = edge_copy(edge_bottom, above, 1, s + 1)

    def send_edges():
        pl.semaphore_wait(barrier, total_greets)
        when(has_above, to_above.start)
        when(has_below, to_below.start)

    lane = iota((8, cols), 1)
    row8 = iota((8, cols), 0)

    def fields(z):
        here = vol[z].astype(F32)
        return here, [here[8 * t:8 * t + 8] for t in range(tiles)]

    def put_second(z, t, grad_rows, far, near):
        grad_depth = 0.5 * (far[8 * t:8 * t + 8] - near[8 * t:8 * t + 8])
        feat[z, t, 16:32] = jnp.concatenate([grad_rows, grad_depth], 0).astype(BF16)

    def near_far(z):
        far = vol[jnp.minimum(z + 1, layers - 1)].astype(F32)
        near = vol[jnp.maximum(z - 1, 0)].astype(F32)
        return far, near

    def vertical(parts, t, first, last):
        lower = parts[t + 1] if t + 1 < tiles else None
        upper = parts[t - 1] if t > 0 else None
        below_row = pltpu.roll(lower, 7, 0) if lower is not None else last
        above_row = pltpu.roll(upper, 1, 0) if upper is not None else first
        following = jnp.where(row8 == 7, below_row, pltpu.roll(parts[t], 7, 0))
        previous = jnp.where(row8 == 0, above_row, pltpu.roll(parts[t], 1, 0))
        return 0.5 * (following - previous)

    ones = jnp.ones((16, cols), BF16)

    def inner_features(z, carry):
        here, parts = fields(z)
        far, near = near_far(z)
        for t in range(tiles):
            right = jnp.where(lane == cols - 1, 0.0, pltpu.roll(parts[t], cols - 1, 1))
            left = jnp.where(lane == 0, 0.0, pltpu.roll(parts[t], 1, 1))
            feat[z, t, 0:16] = jnp.concatenate([parts[t], 0.5 * (right - left)], 0).astype(BF16)
            if 0 < t < tiles - 1:
                put_second(z, t, vertical(parts, t, None, None), far, near)
            feat[z, t, 32:48] = ones
        return carry

    lax.fori_loop(0, layers, inner_features, 0)

    def outer_features(z, carry):
        here, parts = fields(z)
        far, near = near_far(z)
        first = jnp.broadcast_to(above[pl.ds(z, 1)], (8, cols))
        last = jnp.broadcast_to(below[pl.ds(z, 1)], (8, cols))
        for t in (0, tiles - 1):
            put_second(z, t, vertical(parts, t, first, last), far, near)
        return carry

    def finish_features():
        when(has_above, to_below.wait_recv)
        when(has_below, to_above.wait_recv)
        lax.fori_loop(0, layers, outer_features, 0)

    def place(m):
        second = m >= chunks
        c = lax.rem(m, chunks)
        return c, [jnp.where(second, 0, 1), jnp.where(second, tiles - 1, 2)]

    def both(now, z, fresh, before, ready):
        if fresh is not None:
            c, at_tiles = now
            at = pl.multiple_of(c * WIDE, WIDE)
        c2, into, to_tiles = before
        cover = jnp.concatenate(
            [
                jnp.full((8, brick), occ_ref[c2 * (WIDE // brick) + b].astype(F32))
                for b in range(WIDE // brick)
            ],
            1,
        )
        outs = [[], []]
        for p in range(2):
            if fresh is not None:
                for t in range(2):
                    x = feat[z, at_tiles[t], :, pl.ds(at, WIDE)]
                    u = jnp.dot(lhs[p * half:(p + 1) * half], x, preferred_element_type=F32)
                    fresh[t, p] = (u + u * jnp.tanh(u)).astype(BF16)
            for t in range(2):
                outs[t].append(jnp.dot(mix[p], ready[t, p], preferred_element_type=F32))
        for t in range(2):
            out = outs[t][0] + outs[t][1]
            raw = out[24:32] + out_bias[3]
            density = jnp.maximum(raw, 0.0) + jnp.log(1.0 + jnp.exp(-jnp.abs(raw)))
            keep = jnp.exp(-optical * (density * cover))
            here = pl.ds(pl.multiple_of(8 * to_tiles[t], 8), 8)
            glow = [jnp.tanh(out[8 * i:8 * i + 8] + out_bias[i]) for i in range(3)]
            for w in range(2):
                lanes = slice(w * LANES, (w + 1) * LANES)
                remaining = part[into, 3, w, here]
                weight = 0.5 * (remaining * (1.0 - keep[:, lanes]))
                for i in range(3):
                    part[into, i, w, here] = part[into, i, w, here] + (weight + weight * glow[i][:, lanes])
                part[into, 3, w, here] = remaining * keep[:, lanes]

    own_order = order_ref[d]

    def swap(r, c):
        return pltpu.make_async_remote_copy(
            src_ref=sends[r].at[c], dst_ref=receives[r].at[c],
            send_sem=swap_send.at[r, c], recv_sem=swap_recv.at[r, c],
            device_id=(s, d ^ (1 << r)), device_id_type=MESH,
        )

    def pic_copy(c, which, target, strip, depth):
        at = pl.ds(pl.multiple_of(c * WIDE, WIDE), WIDE)
        return pltpu.make_async_remote_copy(
            src_ref=pic.at[:, :, at], dst_ref=target.at[:, :, at],
            send_sem=pic_send.at[which, c], recv_sem=pic_recv.at[which, c],
            device_id=(strip, depth), device_id_type=MESH,
        )

    def pic_copies(c):
        return [
            (None, None, pic_copy(c, 0, up, s, next_d)),
            (None, None, pic_copy(c, 1, down, s, last_d)),
            (corner_below, corner_above, pic_copy(c, 2, up_strip, s + 1, 0)),
            (corner_above, corner_below, pic_copy(c, 3, down_strip, s - 1, depths - 1)),
        ]

    def split(ref, c, i, w, r):
        count = rows >> (r + 1)
        even = ref[c, i, w, pl.ds(0, count, stride=2)]
        odd = ref[c, i, w, pl.ds(1, count, stride=2)]
        mine_odd = ((d >> r) & 1) == 1
        return jnp.where(mine_odd, odd, even), jnp.where(mine_odd, even, odd)

    def progress(r, c):
        source = part if r <= 1 else currents[r - 2]
        if r > 0:
            swap(r - 1, c).wait_recv()
            in_front = ((own_order >> (r - 1)) & 1) == 0
            for w in range(2):
                mine = [split(source, c, i, w, r - 1)[0] for i in range(4)]
                theirs = [receives[r - 1][c, i, w] for i in range(4)]
                fresh = over(in_front, mine, theirs)
                if r < rounds:
                    for i in range(4):
                        currents[r - 1][c, i, w] = fresh[i]
                else:
                    at = pl.ds(pl.multiple_of(c * WIDE + w * LANES, LANES), LANES)
                    for i in range(3):
                        pic[i, 0:share, at] = fresh[i]
        if r < rounds:
            source = part if r == 0 else currents[r - 1]
            for i in range(4):
                for w in range(2):
                    sends[r][c, i, w] = split(source, c, i, w, r)[1]
            swap(r, c).start()
        else:
            for sending, unused, copy in pic_copies(c):
                when(sending, copy.start)

    def advance(m):
        for r in range(rounds, -1, -1):
            c = m - 1 - chunks - gap * r

            @pl.when(c >= 0)
            def _():
                progress(r, c)

    def body(m, carry):
        now = place(m)
        earlier = place(jnp.maximum(m - 1, 0))
        last_layer = (earlier[0], jnp.where(m > 0, earlier[0], chunks), earlier[1])
        this_layer = (now[0], now[0], now[1])
        for z in range(layers):
            fresh, ready = (hid_a, hid_b) if z % 2 == 0 else (hid_b, hid_a)
            both(now, z, fresh, last_layer if z == 0 else this_layer, ready)
        pl.when(m == 0)(send_edges)
        pl.when(m == chunks - 1)(finish_features)
        advance(m)
        return carry

    lax.fori_loop(0, 2 * chunks, body, 0)
    end = place(2 * chunks - 1)
    both(None, None, None, (end[0], end[0], end[1]), hid_b if layers % 2 == 0 else hid_a)
    for m in range(2 * chunks, 2 * chunks + gap * rounds + 1):
        for r in range(rounds, -1, -1):
            if 0 <= m - 1 - chunks - gap * r < chunks:
                progress(r, m - 1 - chunks - gap * r)

    def settle(c, carry):
        for r in range(rounds):
            swap(r, c).wait_send()
        for sending, receiving, copy in pic_copies(c):
            when(sending, copy.wait_send)
            when(receiving, copy.wait_recv)
        return carry

    lax.fori_loop(0, chunks, settle, 0)

    when(has_above, to_above.wait_send)
    when(has_below, to_below.wait_send)
    total = [jnp.full((8, cols), conv_bias_ref[o]) for o in range(3)]
    for i in range(3):
        upper, lower = up[i], down[i]
        first = jnp.where(row8 == 0, pltpu.roll(up_strip[i], (9 - share) % 8, 0), pltpu.roll(upper, 1, 0))
        upper = jnp.where(at_first, first, upper)
        last = jnp.where(row8 == share - 1, pltpu.roll(down_strip[i], share - 1, 0), pltpu.roll(lower, 7, 0))
        lower = jnp.where(at_last, last, lower)
        for a, centre in enumerate((upper, pic[i], lower)):
            left = jnp.where(lane == 0, 0.0, pltpu.roll(centre, 1, 1))
            right = jnp.where(lane == cols - 1, 0.0, pltpu.roll(centre, cols - 1, 1))
            for b, window in enumerate((left, centre, right)):
                for o in range(3):
                    total[o] = total[o] + conv_ref[o, i, a, b] * window
    for o in range(3):
        out_ref[o] = total[o][0:share]


def shards(volume, occupancy, slab_order, w_in, b_in, w_out, b_out, conv_weight, conv_bias):
    strips, depths = lax.axis_size("strip"), lax.axis_size("depth")
    layers, rows, cols = volume.shape
    channels, hidden = w_in.shape
    rounds = depths.bit_length() - 1
    chunks = cols // WIDE
    tiles = rows // 8
    share = rows // depths
    smem = pl.BlockSpec(memory_space=pltpu.SMEM)
    vmem = pl.BlockSpec(memory_space=pltpu.VMEM)
    depth_lhs = channels * 8 + 16
    halves = [pltpu.VMEM((chunks, 4, 2, rows >> (r + 1), LANES), F32) for r in range(rounds)]
    picture = pltpu.VMEM((3, 8, cols), F32)
    edge = pltpu.VMEM((layers, cols), F32)
    dma = pltpu.SemaphoreType.DMA
    result = pl.pallas_call(
        functools.partial(render_kernel, strips, depths, 2),
        out_shape=jax.ShapeDtypeStruct((3, share, cols), F32),
        in_specs=[smem] * 5 + [vmem] * 3 + [pl.BlockSpec(memory_space=pl.ANY)],
        out_specs=vmem,
        scratch_shapes=[
            pltpu.VMEM((layers, rows, cols), BF16),
            pltpu.VMEM((layers, tiles, depth_lhs, cols), BF16),
            pltpu.VMEM((2, 2, 4 * hidden, WIDE), BF16),
            pltpu.VMEM((2, 2, 4 * hidden, WIDE), BF16),
            pltpu.VMEM((8 * hidden, depth_lhs), BF16),
            pltpu.VMEM((2, 32, 4 * hidden), BF16),
            pltpu.VMEM((2, 128, 128), F32),
            pltpu.VMEM((chunks + 1, 4, 2, rows, LANES), F32),
            edge, edge, edge, edge,
            picture, picture, picture, picture, picture,
            *halves, *halves, *halves,
            dma(()), dma((4,)), dma((rounds, chunks)), dma((rounds, chunks)), dma((4, chunks)), dma((4, chunks)),
        ],
        compiler_params=pltpu.CompilerParams(
            collective_id=0, has_side_effects=True, vmem_limit_bytes=60 * 1024 * 1024
        ),
        name="render",
    )(
        occupancy.reshape(-1), slab_order, b_out, conv_weight, conv_bias,
        w_in, b_in.reshape(1, hidden), w_out.T, volume,
    )
    return result.reshape(3, 1, share, 1, cols)


def solution(mesh):
    placed = (P("depth", "strip", None), P("depth", "strip", None)) + (P(),) * 7
    return jax.shard_map(
        shards,
        mesh=mesh,
        in_specs=placed,
        out_specs=P(None, "strip", None, "depth", None),
        check_vma=False,
    )
```

```python
import functools

import jax
import jax.numpy as jnp
from jax import lax
from jax.experimental import pallas as pl
from jax.experimental.pallas import tpu as pltpu
from jax.sharding import PartitionSpec as P

MESH = pl.DeviceIdType.MESH
LANES = 128
WIDE = 2 * LANES
GROUP = 24
F32 = jnp.float32
BF16 = jnp.bfloat16


def iota(shape, dim):
    return lax.broadcasted_iota(jnp.int32, shape, dim)


def over(in_front, mine, theirs):
    front = [jnp.where(in_front, a, b) for a, b in zip(mine, theirs)]
    back = [jnp.where(in_front, b, a) for a, b in zip(mine, theirs)]
    colour = [front[i] + front[3] * back[i] for i in range(3)]
    return colour + [mine[3] * theirs[3]]


def render_kernel(
    strips, depths, gap, groups,
    occ_ref, order_ref, b_out_ref, conv_ref, conv_bias_ref, w_in_ref, b_in_ref, w_out_ref, vol_hbm,
    out_ref,
    vol, feat, hid_a, hid_b, square, part, edge_top, edge_bottom, above, below,
    pic, up, down, up_strip, down_strip, *rest,
):
    rounds = depths.bit_length() - 1
    combs, rest = rest[:len(groups)], rest[len(groups):]
    sends, receives, currents = rest[:rounds], rest[rounds:2 * rounds], rest[2 * rounds:3 * rounds]
    vol_sem, edge_sems, swap_send, swap_recv, pic_send, pic_recv = rest[3 * rounds:]
    layers, rows, cols = vol.shape
    tiles = rows // 8
    hidden = w_in_ref.shape[1]
    chunks = cols // WIDE
    brick = cols // occ_ref.shape[0]
    share = rows // depths
    optical = 2.0 / (layers * depths)
    s = lax.axis_index("strip")
    d = lax.axis_index("depth")

    load = pltpu.make_async_copy(vol_hbm, vol, vol_sem)
    load.start()

    for ref in (above, below):
        ref[...] = jnp.zeros(ref.shape, F32)
    for ref in (up_strip, down_strip, pic):
        ref[...] = jnp.zeros(ref.shape, F32)

    barrier = pltpu.get_barrier_semaphore()

    def greet(strip, depth):
        pl.semaphore_signal(barrier, inc=1, device_id=(strip, depth), device_id_type=MESH)

    next_d = lax.rem(d + 1, depths)
    last_d = lax.rem(d + depths - 1, depths)
    for r in range(rounds):
        greet(s, d ^ (1 << r))
    greet(s, next_d)
    greet(s, last_d)
    has_above, has_below = s > 0, s < strips - 1
    at_first, at_last = d == 0, d == depths - 1
    corner_above = jnp.logical_and(at_first, has_above)
    corner_below = jnp.logical_and(at_last, has_below)

    @pl.when(has_above)
    def _():
        greet(s - 1, d)

    @pl.when(has_below)
    def _():
        greet(s + 1, d)

    @pl.when(corner_above)
    def _():
        greet(s - 1, depths - 1)

    @pl.when(corner_below)
    def _():
        greet(s + 1, 0)

    def when(condition, action):
        if condition is None:
            action()
        else:
            pl.when(condition)(action)

    square[...] = jnp.zeros(square.shape, F32)
    rest_bias = 0.5 * b_in_ref[...]
    square[0, 0:4, 0:hidden] = 0.5 * w_in_ref[...].astype(F32)
    for k in range(3):
        piece = rest_bias.astype(BF16).astype(F32)
        square[0, 4 + k:5 + k, 0:hidden] = piece
        rest_bias = rest_bias - piece
    square[1, 0:4, 0:hidden] = w_out_ref[...].astype(F32)
    turned = square[0].T.astype(BF16)
    out_turned = square[1]
    scale = jnp.where(iota(out_turned.shape, 0) < 3, 0.5, 1.0)
    out_turned = (out_turned * scale).astype(BF16)
    rep = jnp.where(iota((32, 128), 0) // 8 == iota((32, 128), 1), 1.0, 0.0).astype(BF16)
    first_unit = 0
    for comb, units in zip(combs, groups):
        height, width = 8 * units, comb.shape[1]
        expand = iota((height, 128), 0) // 8 + first_unit == iota((height, 128), 1)
        picked = jnp.dot(jnp.where(expand, 1.0, 0.0).astype(BF16), turned, preferred_element_type=F32).astype(BF16)
        k, at = iota((128, width), 0), iota((128, width), 1) - height
        chosen = jnp.logical_or(
            jnp.logical_and(k < 4, jnp.logical_and(at >= 8 * k, at < 8 * k + 8)),
            jnp.logical_and(jnp.logical_and(k >= 4, k < 7), at == 28 + k),
        )
        first = jnp.dot(picked, jnp.where(chosen, 1.0, 0.0).astype(BF16), preferred_element_type=F32)
        at, row = iota((height, width), 1) - height, iota((height, width), 0)
        own = jnp.logical_or(at >= 32, at % 8 == row % 8)
        comb[0:height] = jnp.where(own, first, 0.0).astype(BF16)
        unit, at = iota((128, width), 0), iota((128, width), 1)
        chosen = jnp.logical_and(at < height, at // 8 + first_unit == unit)
        spread = jnp.dot(out_turned, jnp.where(chosen, 1.0, 0.0).astype(BF16), preferred_element_type=F32)
        second = jnp.dot(rep, spread.astype(BF16), preferred_element_type=F32)
        own = iota((32, width), 1) % 8 == iota((32, width), 0) % 8
        comb[height:height + 32] = jnp.where(own, second, 0.0).astype(BF16)
        first_unit += units
    hid_a[...] = jnp.zeros(hid_a.shape, BF16)
    hid_b[...] = jnp.zeros(hid_b.shape, BF16)
    out_bias = [b_out_ref[i] * (0.5 if i < 3 else 1.0) for i in range(4)]

    def clear(c, carry):
        part[c, 0:3] = jnp.zeros((3, 2, rows, LANES), F32)
        part[c, 3] = jnp.ones((2, rows, LANES), F32)
        return carry

    lax.fori_loop(0, chunks, clear, 0)
    load.wait()

    def edges(z, carry):
        edge_top[pl.ds(z, 1)] = vol[z, 0:16].astype(F32)[0:1]
        edge_bottom[pl.ds(z, 1)] = vol[z, rows - 16:rows].astype(F32)[15:16]
        return carry

    lax.fori_loop(0, layers, edges, 0)
    total_greets = (
        rounds + 2 + has_above.astype(jnp.int32) + has_below.astype(jnp.int32)
        + corner_above.astype(jnp.int32) + corner_below.astype(jnp.int32)
    )

    def edge_copy(source, target, which, strip):
        return pltpu.make_async_remote_copy(
            src_ref=source, dst_ref=target, send_sem=edge_sems.at[which], recv_sem=edge_sems.at[which + 2],
            device_id=(strip, d), device_id_type=MESH,
        )

    to_above = edge_copy(edge_top, below, 0, s - 1)
    to_below = edge_copy(edge_bottom, above, 1, s + 1)

    def send_edges():
        pl.semaphore_wait(barrier, total_greets)
        when(has_above, to_above.start)
        when(has_below, to_below.start)

    lane = iota((8, cols), 1)
    row8 = iota((8, cols), 0)

    def fields(z):
        here = vol[z].astype(F32)
        return here, [here[8 * t:8 * t + 8] for t in range(tiles)]

    def put_second(z, t, grad_rows, far, near):
        grad_depth = 0.5 * (far[8 * t:8 * t + 8] - near[8 * t:8 * t + 8])
        feat[z, t, 16:32] = jnp.concatenate([grad_rows, grad_depth], 0).astype(BF16)

    def near_far(z):
        far = vol[jnp.minimum(z + 1, layers - 1)].astype(F32)
        near = vol[jnp.maximum(z - 1, 0)].astype(F32)
        return far, near

    def vertical(parts, t, first, last):
        lower = parts[t + 1] if t + 1 < tiles else None
        upper = parts[t - 1] if t > 0 else None
        below_row = pltpu.roll(lower, 7, 0) if lower is not None else last
        above_row = pltpu.roll(upper, 1, 0) if upper is not None else first
        following = jnp.where(row8 == 7, below_row, pltpu.roll(parts[t], 7, 0))
        previous = jnp.where(row8 == 0, above_row, pltpu.roll(parts[t], 1, 0))
        return 0.5 * (following - previous)

    ones = jnp.ones((16, cols), BF16)

    def inner_features(z, carry):
        here, parts = fields(z)
        far, near = near_far(z)
        for t in range(tiles):
            right = jnp.where(lane == cols - 1, 0.0, pltpu.roll(parts[t], cols - 1, 1))
            left = jnp.where(lane == 0, 0.0, pltpu.roll(parts[t], 1, 1))
            feat[z, t, 0:16] = jnp.concatenate([parts[t], 0.5 * (right - left)], 0).astype(BF16)
            if 0 < t < tiles - 1:
                put_second(z, t, vertical(parts, t, None, None), far, near)
            feat[z, t, 32:48] = ones
        return carry

    lax.fori_loop(0, layers, inner_features, 0)

    def outer_features(z, carry):
        here, parts = fields(z)
        far, near = near_far(z)
        first = jnp.broadcast_to(above[pl.ds(z, 1)], (8, cols))
        last = jnp.broadcast_to(below[pl.ds(z, 1)], (8, cols))
        for t in (0, tiles - 1):
            put_second(z, t, vertical(parts, t, first, last), far, near)
        return carry

    def finish_features():
        when(has_above, to_below.wait_recv)
        when(has_below, to_above.wait_recv)
        lax.fori_loop(0, layers, outer_features, 0)

    ahead = min(4, chunks)

    def place(m):
        paired = m - 2 * ahead >= 0
        second = jnp.where(paired, lax.rem(m, 2) == 1, m >= ahead)
        c = jnp.where(paired, m // 2, jnp.where(second, m - ahead, m))
        return c, [jnp.where(second, 0, 1), jnp.where(second, tiles - 1, 2)]

    def both(now, z, fresh, before, ready):
        c, at_tiles = now
        at = pl.multiple_of(c * WIDE, WIDE)
        c2, into, to_tiles = before
        cover = jnp.concatenate(
            [
                jnp.full((8, brick), occ_ref[c2 * (WIDE // brick) + b].astype(F32))
                for b in range(WIDE // brick)
            ],
            1,
        )
        outs = [[], []]
        start = 0
        for comb, units in zip(combs, groups):
            height = 8 * units
            for t in range(2):
                x = feat[z, at_tiles[t], :, pl.ds(at, WIDE)]
                stacked = jnp.concatenate([ready[t, start:start + height], x], 0)
                if fresh is None:
                    outs[t].append(jnp.dot(comb[height:height + 32], stacked, preferred_element_type=F32))
                    continue
                both_layers = jnp.dot(comb[...], stacked, preferred_element_type=F32)
                u = both_layers[0:height]
                fresh[t, start:start + height] = (u + u * jnp.tanh(u)).astype(BF16)
                outs[t].append(both_layers[height:height + 32])
            start += height
        for t in range(2):
            out = functools.reduce(jnp.add, outs[t])
            raw = out[24:32] + out_bias[3]
            density = jnp.maximum(raw, 0.0) + jnp.log(1.0 + jnp.exp(-jnp.abs(raw)))
            keep = jnp.exp(-optical * (density * cover))
            here = pl.ds(pl.multiple_of(8 * to_tiles[t], 8), 8)
            glow = [jnp.tanh(out[8 * i:8 * i + 8] + out_bias[i]) for i in range(3)]
            for w in range(2):
                lanes = slice(w * LANES, (w + 1) * LANES)
                remaining = part[into, 3, w, here]
                weight = 0.5 * (remaining * (1.0 - keep[:, lanes]))
                for i in range(3):
                    part[into, i, w, here] = part[into, i, w, here] + (weight + weight * glow[i][:, lanes])
                part[into, 3, w, here] = remaining * keep[:, lanes]

    own_order = order_ref[d]

    def swap(r, c):
        return pltpu.make_async_remote_copy(
            src_ref=sends[r].at[c], dst_ref=receives[r].at[c],
            send_sem=swap_send.at[r, c], recv_sem=swap_recv.at[r, c],
            device_id=(s, d ^ (1 << r)), device_id_type=MESH,
        )

    def pic_copy(c, which, target, strip, depth):
        at = pl.ds(pl.multiple_of(c * WIDE, WIDE), WIDE)
        return pltpu.make_async_remote_copy(
            src_ref=pic.at[:, :, at], dst_ref=target.at[:, :, at],
            send_sem=pic_send.at[which, c], recv_sem=pic_recv.at[which, c],
            device_id=(strip, depth), device_id_type=MESH,
        )

    def pic_copies(c):
        return [
            (None, None, pic_copy(c, 0, up, s, next_d)),
            (None, None, pic_copy(c, 1, down, s, last_d)),
            (corner_below, corner_above, pic_copy(c, 2, up_strip, s + 1, 0)),
            (corner_above, corner_below, pic_copy(c, 3, down_strip, s - 1, depths - 1)),
        ]

    def split(ref, c, i, w, r):
        count = rows >> (r + 1)
        even = ref[c, i, w, pl.ds(0, count, stride=2)]
        odd = ref[c, i, w, pl.ds(1, count, stride=2)]
        mine_odd = ((d >> r) & 1) == 1
        return jnp.where(mine_odd, odd, even), jnp.where(mine_odd, even, odd)

    def progress(r, c):
        source = part if r <= 1 else currents[r - 2]
        if r > 0:
            swap(r - 1, c).wait_recv()
            in_front = ((own_order >> (r - 1)) & 1) == 0
            for w in range(2):
                mine = [split(source, c, i, w, r - 1)[0] for i in range(4)]
                theirs = [receives[r - 1][c, i, w] for i in range(4)]
                fresh = over(in_front, mine, theirs)
                if r < rounds:
                    for i in range(4):
                        currents[r - 1][c, i, w] = fresh[i]
                else:
                    at = pl.ds(pl.multiple_of(c * WIDE + w * LANES, LANES), LANES)
                    for i in range(3):
                        pic[i, 0:share, at] = fresh[i]
        if r < rounds:
            source = part if r == 0 else currents[r - 1]
            for i in range(4):
                for w in range(2):
                    sends[r][c, i, w] = split(source, c, i, w, r)[1]
            swap(r, c).start()
        else:
            for sending, unused, copy in pic_copies(c):
                when(sending, copy.start)

    lag = [0] + [2 + gap * r for r in range(rounds)]

    def advance(m):
        for r in range(rounds, -1, -1):
            ended = m - 1 - lag[r]
            early = ended - 2 * ahead < 0
            c = jnp.where(early, ended - ahead, ended // 2)

            @pl.when(jnp.logical_and(ended >= ahead, jnp.logical_or(early, lax.rem(ended, 2) == 1)))
            def _():
                progress(r, c)

    def body(m, carry):
        now = place(m)
        earlier = place(jnp.maximum(m - 1, 0))
        last_layer = (earlier[0], jnp.where(m > 0, earlier[0], chunks), earlier[1])
        this_layer = (now[0], now[0], now[1])
        for z in range(layers):
            hid = hid_a if z % 2 == 0 else hid_b
            both(now, z, hid, last_layer if z < 2 else this_layer, hid)
        pl.when(m == 0)(send_edges)
        pl.when(m == ahead - 1)(finish_features)
        advance(m)
        return carry

    lax.fori_loop(0, 2 * chunks, body, 0)
    end = place(2 * chunks - 1)
    both(end, 0, None, (end[0], end[0], end[1]), hid_a)
    both(end, 0, None, (end[0], end[0], end[1]), hid_b)
    ends = [ahead + c if c < ahead else 2 * c + 1 for c in range(chunks)]
    done = [sum(e + 1 + lag[r] < 2 * chunks for e in ends) for r in range(rounds + 1)]
    progress(0, chunks - 1)
    for r in range(rounds, 0, -1):
        while done[r] < done[r - 1]:
            progress(r, done[r])
            done[r] += 1
    done[0] = chunks
    for r in range(1, rounds + 1):
        for c in range(done[r], chunks):
            progress(r, c)

    def settle(c, carry):
        for r in range(rounds):
            swap(r, c).wait_send()
        for sending, receiving, copy in pic_copies(c):
            when(sending, copy.wait_send)
            when(receiving, copy.wait_recv)
        return carry

    lax.fori_loop(0, chunks, settle, 0)

    when(has_above, to_above.wait_send)
    when(has_below, to_below.wait_send)
    total = [jnp.full((8, cols), conv_bias_ref[o]) for o in range(3)]
    for i in range(3):
        upper, lower = up[i], down[i]
        first = jnp.where(row8 == 0, pltpu.roll(up_strip[i], (9 - share) % 8, 0), pltpu.roll(upper, 1, 0))
        upper = jnp.where(at_first, first, upper)
        last = jnp.where(row8 == share - 1, pltpu.roll(down_strip[i], share - 1, 0), pltpu.roll(lower, 7, 0))
        lower = jnp.where(at_last, last, lower)
        for a, centre in enumerate((upper, pic[i], lower)):
            left = jnp.where(lane == 0, 0.0, pltpu.roll(centre, 1, 1))
            right = jnp.where(lane == cols - 1, 0.0, pltpu.roll(centre, cols - 1, 1))
            for b, window in enumerate((left, centre, right)):
                for o in range(3):
                    total[o] = total[o] + conv_ref[o, i, a, b] * window
    for o in range(3):
        out_ref[o] = total[o][0:share]


def shards(volume, occupancy, slab_order, w_in, b_in, w_out, b_out, conv_weight, conv_bias):
    strips, depths = lax.axis_size("strip"), lax.axis_size("depth")
    layers, rows, cols = volume.shape
    channels, hidden = w_in.shape
    rounds = depths.bit_length() - 1
    chunks = cols // WIDE
    tiles = rows // 8
    share = rows // depths
    smem = pl.BlockSpec(memory_space=pltpu.SMEM)
    vmem = pl.BlockSpec(memory_space=pltpu.VMEM)
    depth_lhs = channels * 8 + 16
    groups = [min(GROUP, hidden - start) for start in range(0, hidden, GROUP)]
    halves = [pltpu.VMEM((chunks, 4, 2, rows >> (r + 1), LANES), F32) for r in range(rounds)]
    picture = pltpu.VMEM((3, 8, cols), F32)
    edge = pltpu.VMEM((layers, cols), F32)
    dma = pltpu.SemaphoreType.DMA
    result = pl.pallas_call(
        functools.partial(render_kernel, strips, depths, 3, groups),
        out_shape=jax.ShapeDtypeStruct((3, share, cols), F32),
        in_specs=[smem] * 5 + [vmem] * 3 + [pl.BlockSpec(memory_space=pl.ANY)],
        out_specs=vmem,
        scratch_shapes=[
            pltpu.VMEM((layers, rows, cols), BF16),
            pltpu.VMEM((layers, tiles, depth_lhs, cols), BF16),
            pltpu.VMEM((2, 8 * hidden, WIDE), BF16),
            pltpu.VMEM((2, 8 * hidden, WIDE), BF16),
            pltpu.VMEM((2, 128, 128), F32),
            pltpu.VMEM((chunks + 1, 4, 2, rows, LANES), F32),
            edge, edge, edge, edge,
            picture, picture, picture, picture, picture,
            *[pltpu.VMEM((8 * units + 32, 8 * units + depth_lhs), BF16) for units in groups],
            *halves, *halves, *halves,
            dma(()), dma((4,)), dma((rounds, chunks)), dma((rounds, chunks)), dma((4, chunks)), dma((4, chunks)),
        ],
        compiler_params=pltpu.CompilerParams(
            collective_id=0, has_side_effects=True, vmem_limit_bytes=60 * 1024 * 1024
        ),
        name="render",
    )(
        occupancy.reshape(-1), slab_order, b_out, conv_weight, conv_bias,
        w_in, b_in.reshape(1, hidden), w_out.T, volume,
    )
    return result.reshape(3, 1, share, 1, cols)


def solution(mesh):
    placed = (P("depth", "strip", None), P("depth", "strip", None)) + (P(),) * 7
    return jax.shard_map(
        shards,
        mesh=mesh,
        in_specs=placed,
        out_specs=P(None, "strip", None, "depth", None),
        check_vma=False,
    )
```

```python
import functools

import jax
import jax.numpy as jnp
from jax import lax
from jax.experimental import pallas as pl
from jax.experimental.pallas import tpu as pltpu
from jax.sharding import PartitionSpec as P

MESH = pl.DeviceIdType.MESH
LANES = 128
WIDE = 2 * LANES
GROUP = 24
F32 = jnp.float32
BF16 = jnp.bfloat16


def iota(shape, dim):
    return lax.broadcasted_iota(jnp.int32, shape, dim)


def over(in_front, mine, theirs):
    front = [jnp.where(in_front, a, b) for a, b in zip(mine, theirs)]
    back = [jnp.where(in_front, b, a) for a, b in zip(mine, theirs)]
    colour = [front[i] + front[3] * back[i] for i in range(3)]
    return colour + [mine[3] * theirs[3]]


def render_kernel(
    strips, depths, gap, groups,
    occ_ref, order_ref, b_out_ref, conv_ref, conv_bias_ref, w_in_ref, b_in_ref, w_out_ref, vol_hbm,
    out_ref,
    vol, feat, hid_a, hid_b, square, part, edge_top, edge_bottom, above, below,
    pic, up, down, up_strip, down_strip, *rest,
):
    rounds = depths.bit_length() - 1
    combs, rest = rest[:len(groups)], rest[len(groups):]
    sends, receives, currents = rest[:rounds], rest[rounds:2 * rounds], rest[2 * rounds:3 * rounds]
    vol_sem, edge_sems, swap_send, swap_recv, pic_send, pic_recv = rest[3 * rounds:]
    layers, rows, cols = vol.shape
    tiles = rows // 8
    hidden = w_in_ref.shape[1]
    chunks = cols // WIDE
    brick = cols // occ_ref.shape[0]
    share = rows // depths
    optical = 2.0 / (layers * depths)
    s = lax.axis_index("strip")
    d = lax.axis_index("depth")

    load = pltpu.make_async_copy(vol_hbm, vol, vol_sem)
    load.start()

    for ref in (above, below):
        ref[...] = jnp.zeros(ref.shape, F32)
    for ref in (up_strip, down_strip, pic):
        ref[...] = jnp.zeros(ref.shape, F32)

    barrier = pltpu.get_barrier_semaphore()

    def greet(strip, depth):
        pl.semaphore_signal(barrier, inc=1, device_id=(strip, depth), device_id_type=MESH)

    next_d = lax.rem(d + 1, depths)
    last_d = lax.rem(d + depths - 1, depths)
    for r in range(rounds):
        greet(s, d ^ (1 << r))
    greet(s, next_d)
    greet(s, last_d)
    has_above, has_below = s > 0, s < strips - 1
    at_first, at_last = d == 0, d == depths - 1
    corner_above = jnp.logical_and(at_first, has_above)
    corner_below = jnp.logical_and(at_last, has_below)

    @pl.when(has_above)
    def _():
        greet(s - 1, d)

    @pl.when(has_below)
    def _():
        greet(s + 1, d)

    @pl.when(corner_above)
    def _():
        greet(s - 1, depths - 1)

    @pl.when(corner_below)
    def _():
        greet(s + 1, 0)

    def when(condition, action):
        if condition is None:
            action()
        else:
            pl.when(condition)(action)

    square[...] = jnp.zeros(square.shape, F32)
    rest_bias = 0.5 * b_in_ref[...]
    square[0, 0:4, 0:hidden] = 0.5 * w_in_ref[...].astype(F32)
    for k in range(3):
        piece = rest_bias.astype(BF16).astype(F32)
        square[0, 4 + k:5 + k, 0:hidden] = piece
        rest_bias = rest_bias - piece
    square[1, 0:4, 0:hidden] = w_out_ref[...].astype(F32)
    turned = square[0].T.astype(BF16)
    out_turned = square[1]
    scale = jnp.where(iota(out_turned.shape, 0) < 3, 0.5, 1.0)
    out_turned = (out_turned * scale).astype(BF16)
    rep = jnp.where(iota((32, 128), 0) // 8 == iota((32, 128), 1), 1.0, 0.0).astype(BF16)
    first_unit = 0
    for comb, units in zip(combs, groups):
        height, width = 8 * units, comb.shape[1]
        expand = iota((height, 128), 0) // 8 + first_unit == iota((height, 128), 1)
        picked = jnp.dot(jnp.where(expand, 1.0, 0.0).astype(BF16), turned, preferred_element_type=F32).astype(BF16)
        k, at = iota((128, width), 0), iota((128, width), 1) - height
        chosen = jnp.logical_or(
            jnp.logical_and(k < 4, jnp.logical_and(at >= 8 * k, at < 8 * k + 8)),
            jnp.logical_and(jnp.logical_and(k >= 4, k < 7), at == 28 + k),
        )
        first = jnp.dot(picked, jnp.where(chosen, 1.0, 0.0).astype(BF16), preferred_element_type=F32)
        at, row = iota((height, width), 1) - height, iota((height, width), 0)
        own = jnp.logical_or(at >= 32, at % 8 == row % 8)
        comb[0:height] = jnp.where(own, first, 0.0).astype(BF16)
        unit, at = iota((128, width), 0), iota((128, width), 1)
        chosen = jnp.logical_and(at < height, at // 8 + first_unit == unit)
        spread = jnp.dot(out_turned, jnp.where(chosen, 1.0, 0.0).astype(BF16), preferred_element_type=F32)
        second = jnp.dot(rep, spread.astype(BF16), preferred_element_type=F32)
        own = iota((32, width), 1) % 8 == iota((32, width), 0) % 8
        comb[height:height + 32] = jnp.where(own, second, 0.0).astype(BF16)
        first_unit += units
    hid_a[...] = jnp.zeros(hid_a.shape, BF16)
    hid_b[...] = jnp.zeros(hid_b.shape, BF16)
    out_bias = [b_out_ref[i] * (0.5 if i < 3 else 1.0) for i in range(4)]

    def clear(c, carry):
        part[c, 0:3] = jnp.zeros((3, 2, rows, LANES), F32)
        part[c, 3] = jnp.ones((2, rows, LANES), F32)
        return carry

    lax.fori_loop(0, chunks, clear, 0)
    load.wait()

    def edges(z, carry):
        edge_top[pl.ds(z, 1)] = vol[z, 0:16].astype(F32)[0:1]
        edge_bottom[pl.ds(z, 1)] = vol[z, rows - 16:rows].astype(F32)[15:16]
        return carry

    lax.fori_loop(0, layers, edges, 0)
    total_greets = (
        rounds + 2 + has_above.astype(jnp.int32) + has_below.astype(jnp.int32)
        + corner_above.astype(jnp.int32) + corner_below.astype(jnp.int32)
    )

    def edge_copy(source, target, which, strip):
        return pltpu.make_async_remote_copy(
            src_ref=source, dst_ref=target, send_sem=edge_sems.at[which], recv_sem=edge_sems.at[which + 2],
            device_id=(strip, d), device_id_type=MESH,
        )

    to_above = edge_copy(edge_top, below, 0, s - 1)
    to_below = edge_copy(edge_bottom, above, 1, s + 1)

    def send_edges():
        pl.semaphore_wait(barrier, total_greets)
        when(has_above, to_above.start)
        when(has_below, to_below.start)

    lane = iota((8, cols), 1)
    row8 = iota((8, cols), 0)

    def fields(z):
        here = vol[z].astype(F32)
        return here, [here[8 * t:8 * t + 8] for t in range(tiles)]

    def put_second(z, t, grad_rows, far, near):
        grad_depth = 0.5 * (far[8 * t:8 * t + 8] - near[8 * t:8 * t + 8])
        feat[z, t, 16:32] = jnp.concatenate([grad_rows, grad_depth], 0).astype(BF16)

    def near_far(z):
        far = vol[jnp.minimum(z + 1, layers - 1)].astype(F32)
        near = vol[jnp.maximum(z - 1, 0)].astype(F32)
        return far, near

    def vertical(parts, t, first, last):
        lower = parts[t + 1] if t + 1 < tiles else None
        upper = parts[t - 1] if t > 0 else None
        below_row = pltpu.roll(lower, 7, 0) if lower is not None else last
        above_row = pltpu.roll(upper, 1, 0) if upper is not None else first
        following = jnp.where(row8 == 7, below_row, pltpu.roll(parts[t], 7, 0))
        previous = jnp.where(row8 == 0, above_row, pltpu.roll(parts[t], 1, 0))
        return 0.5 * (following - previous)

    ones = jnp.ones((16, cols), BF16)

    def inner_features(z, carry):
        here, parts = fields(z)
        far, near = near_far(z)
        for t in range(tiles):
            right = jnp.where(lane == cols - 1, 0.0, pltpu.roll(parts[t], cols - 1, 1))
            left = jnp.where(lane == 0, 0.0, pltpu.roll(parts[t], 1, 1))
            feat[z, t, 0:16] = jnp.concatenate([parts[t], 0.5 * (right - left)], 0).astype(BF16)
            if 0 < t < tiles - 1:
                put_second(z, t, vertical(parts, t, None, None), far, near)
            feat[z, t, 32:48] = ones
        return carry

    lax.fori_loop(0, layers, inner_features, 0)

    def outer_features(z, carry):
        here, parts = fields(z)
        far, near = near_far(z)
        first = jnp.broadcast_to(above[pl.ds(z, 1)], (8, cols))
        last = jnp.broadcast_to(below[pl.ds(z, 1)], (8, cols))
        for t in (0, tiles - 1):
            put_second(z, t, vertical(parts, t, first, last), far, near)
        return carry

    def finish_features():
        when(has_above, to_below.wait_recv)
        when(has_below, to_above.wait_recv)
        lax.fori_loop(0, layers, outer_features, 0)

    ahead = min(4, chunks)

    def place(m):
        paired = m - 2 * ahead >= 0
        second = jnp.where(paired, lax.rem(m, 2) == 1, m >= ahead)
        c = jnp.where(paired, m // 2, jnp.where(second, m - ahead, m))
        return c, [jnp.where(second, 0, 1), jnp.where(second, tiles - 1, 2)]

    def both(now, z, fresh, before, ready):
        c, at_tiles = now
        at = pl.multiple_of(c * WIDE, WIDE)
        c2, into, to_tiles = before
        cover = jnp.concatenate(
            [
                jnp.full((8, brick), occ_ref[c2 * (WIDE // brick) + b].astype(F32))
                for b in range(WIDE // brick)
            ],
            1,
        )
        outs = [[], []]
        start = 0
        for comb, units in zip(combs, groups):
            height = 8 * units
            for t in range(2):
                x = feat[z, at_tiles[t], :, pl.ds(at, WIDE)]
                stacked = jnp.concatenate([ready[t, start:start + height], x], 0)
                if fresh is None:
                    outs[t].append(jnp.dot(comb[height:height + 32], stacked, preferred_element_type=F32))
                    continue
                both_layers = jnp.dot(comb[...], stacked, preferred_element_type=F32)
                u = both_layers[0:height]
                fresh[t, start:start + height] = (u + u * jnp.tanh(u)).astype(BF16)
                outs[t].append(both_layers[height:height + 32])
            start += height
        for t in range(2):
            out = functools.reduce(jnp.add, outs[t])
            raw = out[24:32] + out_bias[3]
            density = jnp.maximum(raw, 0.0) + jnp.log(1.0 + jnp.exp(-jnp.abs(raw)))
            keep = jnp.exp(-optical * (density * cover))
            here = pl.ds(pl.multiple_of(8 * to_tiles[t], 8), 8)
            glow = [jnp.tanh(out[8 * i:8 * i + 8] + out_bias[i]) for i in range(3)]
            for w in range(2):
                lanes = slice(w * LANES, (w + 1) * LANES)
                remaining = part[into, 3, w, here]
                weight = 0.5 * (remaining * (1.0 - keep[:, lanes]))
                for i in range(3):
                    part[into, i, w, here] = part[into, i, w, here] + (weight + weight * glow[i][:, lanes])
                part[into, 3, w, here] = remaining * keep[:, lanes]

    own_order = order_ref[d]

    def swap(r, c):
        return pltpu.make_async_remote_copy(
            src_ref=sends[r].at[c], dst_ref=receives[r].at[c],
            send_sem=swap_send.at[r, c], recv_sem=swap_recv.at[r, c],
            device_id=(s, d ^ (1 << r)), device_id_type=MESH,
        )

    def pic_copy(c, which, target, strip, depth):
        at = pl.ds(pl.multiple_of(c * WIDE, WIDE), WIDE)
        return pltpu.make_async_remote_copy(
            src_ref=pic.at[:, :, at], dst_ref=target.at[:, :, at],
            send_sem=pic_send.at[which, c], recv_sem=pic_recv.at[which, c],
            device_id=(strip, depth), device_id_type=MESH,
        )

    def pic_copies(c):
        return [
            (None, None, pic_copy(c, 0, up, s, next_d)),
            (None, None, pic_copy(c, 1, down, s, last_d)),
            (corner_below, corner_above, pic_copy(c, 2, up_strip, s + 1, 0)),
            (corner_above, corner_below, pic_copy(c, 3, down_strip, s - 1, depths - 1)),
        ]

    def split(ref, c, i, w, r):
        count = rows >> (r + 1)
        even = ref[c, i, w, pl.ds(0, count, stride=2)]
        odd = ref[c, i, w, pl.ds(1, count, stride=2)]
        mine_odd = ((d >> r) & 1) == 1
        return jnp.where(mine_odd, odd, even), jnp.where(mine_odd, even, odd)

    def progress(r, c):
        source = part if r <= 1 else currents[r - 2]
        if r > 0:
            swap(r - 1, c).wait_recv()
            in_front = ((own_order >> (r - 1)) & 1) == 0
            for w in range(2):
                mine = [split(source, c, i, w, r - 1)[0] for i in range(4)]
                theirs = [receives[r - 1][c, i, w] for i in range(4)]
                fresh = over(in_front, mine, theirs)
                if r < rounds:
                    for i in range(4):
                        currents[r - 1][c, i, w] = fresh[i]
                else:
                    at = pl.ds(pl.multiple_of(c * WIDE + w * LANES, LANES), LANES)
                    for i in range(3):
                        pic[i, 0:share, at] = fresh[i]
        if r < rounds:
            source = part if r == 0 else currents[r - 1]
            for i in range(4):
                for w in range(2):
                    sends[r][c, i, w] = split(source, c, i, w, r)[1]
            swap(r, c).start()
        else:
            for sending, unused, copy in pic_copies(c):
                when(sending, copy.start)

    lag = [0] + [2 + gap * r for r in range(rounds)]

    def advance(m):
        for r in range(rounds, -1, -1):
            ended = m - 1 - lag[r]
            early = ended - 2 * ahead < 0
            c = jnp.where(early, ended - ahead, ended // 2)

            @pl.when(jnp.logical_and(ended >= ahead, jnp.logical_or(early, lax.rem(ended, 2) == 1)))
            def _():
                progress(r, c)

    def body(m, carry):
        now = place(m)
        earlier = place(jnp.maximum(m - 1, 0))
        last_layer = (earlier[0], jnp.where(m > 0, earlier[0], chunks), earlier[1])
        this_layer = (now[0], now[0], now[1])
        for z in range(layers):
            hid = hid_a if z % 2 == 0 else hid_b
            both(now, z, hid, last_layer if z < 2 else this_layer, hid)
        pl.when(m == 0)(send_edges)
        pl.when(m == ahead - 1)(finish_features)
        advance(m)
        return carry

    lax.fori_loop(0, 2 * chunks, body, 0)
    end = place(2 * chunks - 1)
    both(end, 0, None, (end[0], end[0], end[1]), hid_a)
    both(end, 0, None, (end[0], end[0], end[1]), hid_b)
    ends = [ahead + c if c < ahead else 2 * c + 1 for c in range(chunks)]
    done = [sum(e + 1 + lag[r] < 2 * chunks for e in ends) for r in range(rounds + 1)]
    progress(0, chunks - 1)
    for r in range(rounds, 0, -1):
        while done[r] < done[r - 1]:
            progress(r, done[r])
            done[r] += 1
    done[0] = chunks
    for r in range(1, rounds + 1):
        for c in range(done[r], chunks if r < rounds else chunks - 1):
            progress(r, c)

    def settle(c, carry):
        for r in range(rounds):
            swap(r, c).wait_send()
        for sending, receiving, copy in pic_copies(c):
            when(sending, copy.wait_send)
            when(receiving, copy.wait_recv)
        return carry

    def denoise(low, high, first_col, last_col):
        span = slice(first_col, last_col)
        width = last_col - first_col
        lane, row = iota((8, width), 1), iota((8, width), 0)
        total = [jnp.full((8, width), conv_bias_ref[o]) for o in range(3)]
        for i in range(3):
            upper, lower = up[i, :, span], down[i, :, span]
            first = jnp.where(
                row == 0, pltpu.roll(up_strip[i, :, span], (9 - share) % 8, 0), pltpu.roll(upper, 1, 0)
            )
            upper = jnp.where(at_first, first, upper)
            last = jnp.where(
                row == share - 1, pltpu.roll(down_strip[i, :, span], share - 1, 0), pltpu.roll(lower, 7, 0)
            )
            lower = jnp.where(at_last, last, lower)
            for a, centre in enumerate((upper, pic[i, :, span], lower)):
                left = jnp.where(lane + first_col == 0, 0.0, pltpu.roll(centre, 1, 1))
                right = jnp.where(lane + first_col == cols - 1, 0.0, pltpu.roll(centre, width - 1, 1))
                for b, window in enumerate((left, centre, right)):
                    for o in range(3):
                        total[o] = total[o] + conv_ref[o, i, a, b] * window
        for o in range(3):
            for k in range(share):
                out_ref[o, 0, k, :, low:high] = total[o][k:k + 1, low - first_col:high - first_col]

    middle = chunks // 2 * WIDE
    left_chunks = min(middle // WIDE + 1, chunks - 1)
    lax.fori_loop(0, left_chunks, settle, 0)
    early = (0, middle, 0, middle + LANES)
    if left_chunks * WIDE >= middle + LANES:
        denoise(*early)
    progress(rounds, chunks - 1)
    lax.fori_loop(left_chunks, chunks, settle, 0)
    when(has_above, to_above.wait_send)
    when(has_below, to_below.wait_send)
    if left_chunks * WIDE < middle + LANES:
        denoise(*early)
    denoise(middle, cols, middle - LANES, cols)


def shards(volume, occupancy, slab_order, w_in, b_in, w_out, b_out, conv_weight, conv_bias):
    strips, depths = lax.axis_size("strip"), lax.axis_size("depth")
    layers, rows, cols = volume.shape
    channels, hidden = w_in.shape
    rounds = depths.bit_length() - 1
    chunks = cols // WIDE
    tiles = rows // 8
    share = rows // depths
    smem = pl.BlockSpec(memory_space=pltpu.SMEM)
    vmem = pl.BlockSpec(memory_space=pltpu.VMEM)
    depth_lhs = channels * 8 + 16
    groups = [min(GROUP, hidden - start) for start in range(0, hidden, GROUP)]
    halves = [pltpu.VMEM((chunks, 4, 2, rows >> (r + 1), LANES), F32) for r in range(rounds)]
    picture = pltpu.VMEM((3, 8, cols), F32)
    edge = pltpu.VMEM((layers, cols), F32)
    dma = pltpu.SemaphoreType.DMA
    return pl.pallas_call(
        functools.partial(render_kernel, strips, depths, 3, groups),
        out_shape=jax.ShapeDtypeStruct((3, 1, share, 1, cols), F32),
        in_specs=[smem] * 5 + [vmem] * 3 + [pl.BlockSpec(memory_space=pl.ANY)],
        out_specs=vmem,
        scratch_shapes=[
            pltpu.VMEM((layers, rows, cols), BF16),
            pltpu.VMEM((layers, tiles, depth_lhs, cols), BF16),
            pltpu.VMEM((2, 8 * hidden, WIDE), BF16),
            pltpu.VMEM((2, 8 * hidden, WIDE), BF16),
            pltpu.VMEM((2, 128, 128), F32),
            pltpu.VMEM((chunks + 1, 4, 2, rows, LANES), F32),
            edge, edge, edge, edge,
            picture, picture, picture, picture, picture,
            *[pltpu.VMEM((8 * units + 32, 8 * units + depth_lhs), BF16) for units in groups],
            *halves, *halves, *halves,
            dma(()), dma((4,)), dma((rounds, chunks)), dma((rounds, chunks)), dma((4, chunks)), dma((4, chunks)),
        ],
        compiler_params=pltpu.CompilerParams(
            collective_id=0, has_side_effects=True, vmem_limit_bytes=60 * 1024 * 1024
        ),
        name="render",
    )(
        occupancy.reshape(-1), slab_order, b_out, conv_weight, conv_bias,
        w_in, b_in.reshape(1, hidden), w_out.T, volume,
    )


def solution(mesh):
    placed = (P("depth", "strip", None), P("depth", "strip", None)) + (P(),) * 7
    return jax.shard_map(
        shards,
        mesh=mesh,
        in_specs=placed,
        out_specs=P(None, "strip", None, "depth", None),
        check_vma=False,
    )
```

```python
import functools

import jax
import jax.numpy as jnp
from jax import lax
from jax.experimental import pallas as pl
from jax.experimental.pallas import tpu as pltpu
from jax.sharding import PartitionSpec as P

MESH = pl.DeviceIdType.MESH
LANES = 128
WIDE = 2 * LANES
GROUP = 24
F32 = jnp.float32
BF16 = jnp.bfloat16


def iota(shape, dim):
    return lax.broadcasted_iota(jnp.int32, shape, dim)


def over(in_front, mine, theirs):
    front = [jnp.where(in_front, a, b) for a, b in zip(mine, theirs)]
    back = [jnp.where(in_front, b, a) for a, b in zip(mine, theirs)]
    colour = [front[i] + front[3] * back[i] for i in range(3)]
    return colour + [mine[3] * theirs[3]]


def render_kernel(
    strips, depths, gap, groups,
    occ_ref, order_ref, b_out_ref, conv_ref, conv_bias_ref, w_in_ref, b_in_ref, w_out_ref, vol_hbm,
    out_ref,
    vol, feat, hid_a, hid_b, square, part, edge_top, edge_bottom, above, below,
    pic, up, down, up_strip, down_strip, *rest,
):
    rounds = depths.bit_length() - 1
    combs, rest = rest[:len(groups)], rest[len(groups):]
    sends, receives, currents = rest[:rounds], rest[rounds:2 * rounds], rest[2 * rounds:3 * rounds]
    vol_sem, edge_sems, swap_send, swap_recv, pic_send, pic_recv = rest[3 * rounds:]
    layers, rows, cols = vol.shape
    tiles = rows // 8
    hidden = w_in_ref.shape[1]
    chunks = cols // WIDE
    brick = cols // occ_ref.shape[0]
    share = rows // depths
    optical = 2.0 / (layers * depths)
    s = lax.axis_index("strip")
    d = lax.axis_index("depth")

    load = pltpu.make_async_copy(vol_hbm, vol, vol_sem)
    load.start()

    for ref in (above, below):
        ref[...] = jnp.zeros(ref.shape, F32)
    for ref in (up_strip, down_strip, pic):
        ref[...] = jnp.zeros(ref.shape, F32)

    barrier = pltpu.get_barrier_semaphore()

    def greet(strip, depth):
        pl.semaphore_signal(barrier, inc=1, device_id=(strip, depth), device_id_type=MESH)

    next_d = lax.rem(d + 1, depths)
    last_d = lax.rem(d + depths - 1, depths)
    for r in range(rounds):
        greet(s, d ^ (1 << r))
    greet(s, next_d)
    greet(s, last_d)
    has_above, has_below = s > 0, s < strips - 1
    at_first, at_last = d == 0, d == depths - 1
    corner_above = jnp.logical_and(at_first, has_above)
    corner_below = jnp.logical_and(at_last, has_below)

    @pl.when(has_above)
    def _():
        greet(s - 1, d)

    @pl.when(has_below)
    def _():
        greet(s + 1, d)

    @pl.when(corner_above)
    def _():
        greet(s - 1, depths - 1)

    @pl.when(corner_below)
    def _():
        greet(s + 1, 0)

    def when(condition, action):
        if condition is None:
            action()
        else:
            pl.when(condition)(action)

    square[...] = jnp.zeros(square.shape, F32)
    rest_bias = 0.5 * b_in_ref[...]
    square[0, 0:4, 0:hidden] = 0.5 * w_in_ref[...].astype(F32)
    for k in range(3):
        piece = rest_bias.astype(BF16).astype(F32)
        square[0, 4 + k:5 + k, 0:hidden] = piece
        rest_bias = rest_bias - piece
    square[1, 0:4, 0:hidden] = w_out_ref[...].astype(F32)
    turned = square[0].T.astype(BF16)
    out_turned = square[1]
    scale = jnp.where(iota(out_turned.shape, 0) < 3, 0.5, 1.0)
    out_turned = (out_turned * scale).astype(BF16)
    rep = jnp.where(iota((32, 128), 0) // 8 == iota((32, 128), 1), 1.0, 0.0).astype(BF16)
    first_unit = 0
    for comb, units in zip(combs, groups):
        height, width = 8 * units, comb.shape[1]
        expand = iota((height, 128), 0) // 8 + first_unit == iota((height, 128), 1)
        picked = jnp.dot(jnp.where(expand, 1.0, 0.0).astype(BF16), turned, preferred_element_type=F32).astype(BF16)
        k, at = iota((128, width), 0), iota((128, width), 1) - height
        chosen = jnp.logical_or(
            jnp.logical_and(k < 4, jnp.logical_and(at >= 8 * k, at < 8 * k + 8)),
            jnp.logical_and(jnp.logical_and(k >= 4, k < 7), at == 28 + k),
        )
        first = jnp.dot(picked, jnp.where(chosen, 1.0, 0.0).astype(BF16), preferred_element_type=F32)
        at, row = iota((height, width), 1) - height, iota((height, width), 0)
        own = jnp.logical_or(at >= 32, at % 8 == row % 8)
        comb[0:height] = jnp.where(own, first, 0.0).astype(BF16)
        unit, at = iota((128, width), 0), iota((128, width), 1)
        chosen = jnp.logical_and(at < height, at // 8 + first_unit == unit)
        spread = jnp.dot(out_turned, jnp.where(chosen, 1.0, 0.0).astype(BF16), preferred_element_type=F32)
        second = jnp.dot(rep, spread.astype(BF16), preferred_element_type=F32)
        own = iota((32, width), 1) % 8 == iota((32, width), 0) % 8
        comb[height:height + 32] = jnp.where(own, second, 0.0).astype(BF16)
        first_unit += units
    hid_a[...] = jnp.zeros(hid_a.shape, BF16)
    hid_b[...] = jnp.zeros(hid_b.shape, BF16)
    out_bias = [b_out_ref[i] * (0.5 if i < 3 else 1.0) for i in range(4)]

    def clear(c, carry):
        part[c, 0:3] = jnp.zeros((3, 2, rows, LANES), F32)
        part[c, 3] = jnp.ones((2, rows, LANES), F32)
        return carry

    lax.fori_loop(0, chunks, clear, 0)
    load.wait()

    def edges(z, carry):
        edge_top[pl.ds(z, 1)] = vol[z, 0:16].astype(F32)[0:1]
        edge_bottom[pl.ds(z, 1)] = vol[z, rows - 16:rows].astype(F32)[15:16]
        return carry

    lax.fori_loop(0, layers, edges, 0)
    total_greets = (
        rounds + 2 + has_above.astype(jnp.int32) + has_below.astype(jnp.int32)
        + corner_above.astype(jnp.int32) + corner_below.astype(jnp.int32)
    )

    def edge_copy(source, target, which, strip):
        return pltpu.make_async_remote_copy(
            src_ref=source, dst_ref=target, send_sem=edge_sems.at[which], recv_sem=edge_sems.at[which + 2],
            device_id=(strip, d), device_id_type=MESH,
        )

    to_above = edge_copy(edge_top, below, 0, s - 1)
    to_below = edge_copy(edge_bottom, above, 1, s + 1)

    def send_edges():
        pl.semaphore_wait(barrier, total_greets)
        when(has_above, to_above.start)
        when(has_below, to_below.start)

    lane = iota((8, cols), 1)
    row8 = iota((8, cols), 0)

    def fields(z):
        here = vol[z].astype(F32)
        return here, [here[8 * t:8 * t + 8] for t in range(tiles)]

    def put_second(z, t, grad_rows, far, near):
        grad_depth = 0.5 * (far[8 * t:8 * t + 8] - near[8 * t:8 * t + 8])
        feat[z, t, 16:32] = jnp.concatenate([grad_rows, grad_depth], 0).astype(BF16)

    def near_far(z):
        far = vol[jnp.minimum(z + 1, layers - 1)].astype(F32)
        near = vol[jnp.maximum(z - 1, 0)].astype(F32)
        return far, near

    def vertical(parts, t, first, last):
        lower = parts[t + 1] if t + 1 < tiles else None
        upper = parts[t - 1] if t > 0 else None
        below_row = pltpu.roll(lower, 7, 0) if lower is not None else last
        above_row = pltpu.roll(upper, 1, 0) if upper is not None else first
        following = jnp.where(row8 == 7, below_row, pltpu.roll(parts[t], 7, 0))
        previous = jnp.where(row8 == 0, above_row, pltpu.roll(parts[t], 1, 0))
        return 0.5 * (following - previous)

    ones = jnp.ones((16, cols), BF16)

    def inner_features(z, carry):
        here, parts = fields(z)
        far, near = near_far(z)
        for t in range(tiles):
            right = jnp.where(lane == cols - 1, 0.0, pltpu.roll(parts[t], cols - 1, 1))
            left = jnp.where(lane == 0, 0.0, pltpu.roll(parts[t], 1, 1))
            feat[z, t, 0:16] = jnp.concatenate([parts[t], 0.5 * (right - left)], 0).astype(BF16)
            if 0 < t < tiles - 1:
                put_second(z, t, vertical(parts, t, None, None), far, near)
            feat[z, t, 32:48] = ones
        return carry

    lax.fori_loop(0, layers, inner_features, 0)

    def outer_features(z, carry):
        here, parts = fields(z)
        far, near = near_far(z)
        first = jnp.broadcast_to(above[pl.ds(z, 1)], (8, cols))
        last = jnp.broadcast_to(below[pl.ds(z, 1)], (8, cols))
        for t in (0, tiles - 1):
            put_second(z, t, vertical(parts, t, first, last), far, near)
        return carry

    def finish_features():
        when(has_above, to_below.wait_recv)
        when(has_below, to_above.wait_recv)
        lax.fori_loop(0, layers, outer_features, 0)

    ahead = min(5, chunks)

    def place(m):
        paired = m - 2 * ahead >= 0
        second = jnp.where(paired, lax.rem(m, 2) == 1, m >= ahead)
        c = jnp.where(paired, m // 2, jnp.where(second, m - ahead, m))
        return c, [jnp.where(second, 0, 1), jnp.where(second, tiles - 1, 2)]

    def both(now, z, fresh, before, ready):
        c, at_tiles = now
        at = pl.multiple_of(c * WIDE, WIDE)
        c2, into, to_tiles = before
        cover = jnp.concatenate(
            [
                jnp.full((8, brick), occ_ref[c2 * (WIDE // brick) + b].astype(F32))
                for b in range(WIDE // brick)
            ],
            1,
        )
        outs = [[], []]
        start = 0
        for comb, units in zip(combs, groups):
            height = 8 * units
            for t in range(2):
                x = feat[z, at_tiles[t], :, pl.ds(at, WIDE)]
                stacked = jnp.concatenate([ready[t, start:start + height], x], 0)
                if fresh is None:
                    outs[t].append(jnp.dot(comb[height:height + 32], stacked, preferred_element_type=F32))
                    continue
                both_layers = jnp.dot(comb[...], stacked, preferred_element_type=F32)
                u = both_layers[0:height]
                fresh[t, start:start + height] = (u + u * jnp.tanh(u)).astype(BF16)
                outs[t].append(both_layers[height:height + 32])
            start += height
        for t in range(2):
            out = functools.reduce(jnp.add, outs[t])
            raw = out[24:32] + out_bias[3]
            density = jnp.maximum(raw, 0.0) + jnp.log(1.0 + jnp.exp(-jnp.abs(raw)))
            keep = jnp.exp(-optical * (density * cover))
            here = pl.ds(pl.multiple_of(8 * to_tiles[t], 8), 8)
            glow = [jnp.tanh(out[8 * i:8 * i + 8] + out_bias[i]) for i in range(3)]
            for w in range(2):
                lanes = slice(w * LANES, (w + 1) * LANES)
                remaining = part[into, 3, w, here]
                weight = 0.5 * (remaining * (1.0 - keep[:, lanes]))
                for i in range(3):
                    part[into, i, w, here] = part[into, i, w, here] + (weight + weight * glow[i][:, lanes])
                part[into, 3, w, here] = remaining * keep[:, lanes]

    own_order = order_ref[d]

    def swap(r, c):
        return pltpu.make_async_remote_copy(
            src_ref=sends[r].at[c], dst_ref=receives[r].at[c],
            send_sem=swap_send.at[r, c], recv_sem=swap_recv.at[r, c],
            device_id=(s, d ^ (1 << r)), device_id_type=MESH,
        )

    def pic_copy(c, which, target, strip, depth):
        at = pl.ds(pl.multiple_of(c * WIDE, WIDE), WIDE)
        return pltpu.make_async_remote_copy(
            src_ref=pic.at[:, :, at], dst_ref=target.at[:, :, at],
            send_sem=pic_send.at[which, c], recv_sem=pic_recv.at[which, c],
            device_id=(strip, depth), device_id_type=MESH,
        )

    def pic_copies(c):
        return [
            (None, None, pic_copy(c, 0, up, s, next_d)),
            (None, None, pic_copy(c, 1, down, s, last_d)),
            (corner_below, corner_above, pic_copy(c, 2, up_strip, s + 1, 0)),
            (corner_above, corner_below, pic_copy(c, 3, down_strip, s - 1, depths - 1)),
        ]

    def split(ref, c, i, w, r):
        count = rows >> (r + 1)
        even = ref[c, i, w, pl.ds(0, count, stride=2)]
        odd = ref[c, i, w, pl.ds(1, count, stride=2)]
        mine_odd = ((d >> r) & 1) == 1
        return jnp.where(mine_odd, odd, even), jnp.where(mine_odd, even, odd)

    def progress(r, c):
        source = part if r <= 1 else currents[r - 2]
        if r > 0:
            swap(r - 1, c).wait_recv()
            in_front = ((own_order >> (r - 1)) & 1) == 0
            for w in range(2):
                mine = [split(source, c, i, w, r - 1)[0] for i in range(4)]
                theirs = [receives[r - 1][c, i, w] for i in range(4)]
                fresh = over(in_front, mine, theirs)
                if r < rounds:
                    for i in range(4):
                        currents[r - 1][c, i, w] = fresh[i]
                else:
                    at = pl.ds(pl.multiple_of(c * WIDE + w * LANES, LANES), LANES)
                    for i in range(3):
                        pic[i, 0:share, at] = fresh[i]
        if r < rounds:
            source = part if r == 0 else currents[r - 1]
            for i in range(4):
                for w in range(2):
                    sends[r][c, i, w] = split(source, c, i, w, r)[1]
            swap(r, c).start()
        else:
            for sending, unused, copy in pic_copies(c):
                when(sending, copy.start)

    lag = [0] + [2 + gap * r for r in range(rounds)]

    def advance(m):
        for r in range(rounds, -1, -1):
            ended = m - 1 - lag[r]
            early = ended - 2 * ahead < 0
            c = jnp.where(early, ended - ahead, ended // 2)

            @pl.when(jnp.logical_and(ended >= ahead, jnp.logical_or(early, lax.rem(ended, 2) == 1)))
            def _():
                progress(r, c)

    def body(m, carry):
        now = place(m)
        earlier = place(jnp.maximum(m - 1, 0))
        last_layer = (earlier[0], jnp.where(m > 0, earlier[0], chunks), earlier[1])
        this_layer = (now[0], now[0], now[1])
        for z in range(layers):
            hid = hid_a if z % 2 == 0 else hid_b
            both(now, z, hid, last_layer if z < 2 else this_layer, hid)
        pl.when(m == 0)(send_edges)
        pl.when(m == ahead - 1)(finish_features)
        advance(m)
        return carry

    lax.fori_loop(0, 2 * chunks, body, 0)
    end = place(2 * chunks - 1)
    both(end, 0, None, (end[0], end[0], end[1]), hid_a)
    both(end, 0, None, (end[0], end[0], end[1]), hid_b)
    ends = [ahead + c if c < ahead else 2 * c + 1 for c in range(chunks)]
    done = [sum(e + 1 + lag[r] < 2 * chunks for e in ends) for r in range(rounds + 1)]
    progress(0, chunks - 1)
    for r in range(rounds, 0, -1):
        while done[r] < done[r - 1]:
            progress(r, done[r])
            done[r] += 1
    done[0] = chunks
    for r in range(1, rounds + 1):
        for c in range(done[r], chunks if r < rounds else chunks - 1):
            progress(r, c)

    def settle(c, carry):
        for r in range(rounds):
            swap(r, c).wait_send()
        for sending, receiving, copy in pic_copies(c):
            when(sending, copy.wait_send)
            when(receiving, copy.wait_recv)
        return carry

    def denoise(low, high, first_col, last_col):
        span = slice(first_col, last_col)
        width = last_col - first_col
        lane, row = iota((8, width), 1), iota((8, width), 0)
        total = [jnp.full((8, width), conv_bias_ref[o]) for o in range(3)]
        for i in range(3):
            upper, lower = up[i, :, span], down[i, :, span]
            first = jnp.where(
                row == 0, pltpu.roll(up_strip[i, :, span], (9 - share) % 8, 0), pltpu.roll(upper, 1, 0)
            )
            upper = jnp.where(at_first, first, upper)
            last = jnp.where(
                row == share - 1, pltpu.roll(down_strip[i, :, span], share - 1, 0), pltpu.roll(lower, 7, 0)
            )
            lower = jnp.where(at_last, last, lower)
            for a, centre in enumerate((upper, pic[i, :, span], lower)):
                left = jnp.where(lane + first_col == 0, 0.0, pltpu.roll(centre, 1, 1))
                right = jnp.where(lane + first_col == cols - 1, 0.0, pltpu.roll(centre, width - 1, 1))
                for b, window in enumerate((left, centre, right)):
                    for o in range(3):
                        total[o] = total[o] + conv_ref[o, i, a, b] * window
        for o in range(3):
            for k in range(share):
                out_ref[o, 0, k, :, low:high] = total[o][k:k + 1, low - first_col:high - first_col]

    middle = chunks // 2 * WIDE
    left_chunks = min(middle // WIDE + 1, chunks - 1)
    lax.fori_loop(0, left_chunks, settle, 0)
    early = (0, middle, 0, middle + LANES)
    if left_chunks * WIDE >= middle + LANES:
        denoise(*early)
    progress(rounds, chunks - 1)
    lax.fori_loop(left_chunks, chunks, settle, 0)
    when(has_above, to_above.wait_send)
    when(has_below, to_below.wait_send)
    if left_chunks * WIDE < middle + LANES:
        denoise(*early)
    denoise(middle, cols, middle - LANES, cols)


def shards(volume, occupancy, slab_order, w_in, b_in, w_out, b_out, conv_weight, conv_bias):
    strips, depths = lax.axis_size("strip"), lax.axis_size("depth")
    layers, rows, cols = volume.shape
    channels, hidden = w_in.shape
    rounds = depths.bit_length() - 1
    chunks = cols // WIDE
    tiles = rows // 8
    share = rows // depths
    smem = pl.BlockSpec(memory_space=pltpu.SMEM)
    vmem = pl.BlockSpec(memory_space=pltpu.VMEM)
    depth_lhs = channels * 8 + 16
    groups = [min(GROUP, hidden - start) for start in range(0, hidden, GROUP)]
    halves = [pltpu.VMEM((chunks, 4, 2, rows >> (r + 1), LANES), F32) for r in range(rounds)]
    picture = pltpu.VMEM((3, 8, cols), F32)
    edge = pltpu.VMEM((layers, cols), F32)
    dma = pltpu.SemaphoreType.DMA
    return pl.pallas_call(
        functools.partial(render_kernel, strips, depths, 3, groups),
        out_shape=jax.ShapeDtypeStruct((3, 1, share, 1, cols), F32),
        in_specs=[smem] * 5 + [vmem] * 3 + [pl.BlockSpec(memory_space=pl.ANY)],
        out_specs=vmem,
        scratch_shapes=[
            pltpu.VMEM((layers, rows, cols), BF16),
            pltpu.VMEM((layers, tiles, depth_lhs, cols), BF16),
            pltpu.VMEM((2, 8 * hidden, WIDE), BF16),
            pltpu.VMEM((2, 8 * hidden, WIDE), BF16),
            pltpu.VMEM((2, 128, 128), F32),
            pltpu.VMEM((chunks + 1, 4, 2, rows, LANES), F32),
            edge, edge, edge, edge,
            picture, picture, picture, picture, picture,
            *[pltpu.VMEM((8 * units + 32, 8 * units + depth_lhs), BF16) for units in groups],
            *halves, *halves, *halves,
            dma(()), dma((4,)), dma((rounds, chunks)), dma((rounds, chunks)), dma((4, chunks)), dma((4, chunks)),
        ],
        compiler_params=pltpu.CompilerParams(
            collective_id=0, has_side_effects=True, vmem_limit_bytes=60 * 1024 * 1024
        ),
        name="render",
    )(
        occupancy.reshape(-1), slab_order, b_out, conv_weight, conv_bias,
        w_in, b_in.reshape(1, hidden), w_out.T, volume,
    )


def solution(mesh):
    placed = (P("depth", "strip", None), P("depth", "strip", None)) + (P(),) * 7
    return jax.shard_map(
        shards,
        mesh=mesh,
        in_specs=placed,
        out_specs=P(None, "strip", None, "depth", None),
        check_vma=False,
    )
```
